32 devices in a mesh: dp: 16 (over z, y, x), tensor: 2 (over core).
Axes of the slice: x: 2, y: 2, z: 4, core: 2. Of those that a mesh axis runs over, the one named last changes fastest.
Arguments:
- tokens: bfloat16 [16, 2, 128, 1152], P('dp', 'tensor'), may hold values from -6 to 6
- cond: bfloat16 [1, 1152], replicated, may hold values from -6 to 6
- out_grad: bfloat16 [16, 2, 128, 1152], P(None, 'tensor', 'dp'), may hold values from -6 to 6
- w_qkv: bfloat16 [2, 1152, 3, 1152], P(None, 'dp', None, 'tensor'), may hold values from -0.1875 to 0.1875
- w_out: bfloat16 [2, 1152, 1152], P(None, 'tensor', 'dp'), may hold values from -0.75 to 0.75
- w_fc1: bfloat16 [2, 1152, 4608], P(None, 'dp', 'tensor'), may hold values from -0.1875 to 0.1875
- w_fc2: bfloat16 [2, 4608, 1152], P(None, 'tensor', 'dp'), may hold values from -0.125 to 0.125
- w_ada: bfloat16 [2, 1152, 6, 1152], P(None, ('dp', 'tensor')), may hold values from -0.1875 to 0.1875
- b_ada: bfloat16 [2, 6, 1152], P(None, None, ('dp', 'tensor')), may hold values from -3 to 3
- b_proj: bfloat16 [2, 4, 1152], P(None, None, ('dp', 'tensor')), may hold values from -3 to 3
- b_fc1: bfloat16 [2, 4608], P(None, ('dp', 'tensor')), may hold values from -3 to 3
Outputs:
- output: bfloat16 [16, 2, 128, 1152], P(None, 'tensor', 'dp')
- tokens_grad: float32 [16, 2, 128, 1152], P('dp', 'tensor')
- cond_grad: float32 [1, 1152], P(None, ('dp', 'tensor'))
- w_qkv_grad: float32 [2, 1152, 3, 1152], P(None, 'dp', None, 'tensor')
- w_out_grad: float32 [2, 1152, 1152], P(None, 'tensor', 'dp')
- w_fc1_grad: float32 [2, 1152, 4608], P(None, 'dp', 'tensor')
- w_fc2_grad: float32 [2, 4608, 1152], P(None, 'tensor', 'dp')
- w_ada_grad: float32 [2, 1152, 6, 1152], P(None, ('dp', 'tensor'))
- b_ada_grad: float32 [2, 6, 1152], P(None, None, ('dp', 'tensor'))
- b_proj_grad: float32 [2, 4, 1152], P(None, None, ('dp', 'tensor'))
- b_fc1_grad: float32 [2, 4608], P(None, ('dp', 'tensor'))
The draws below stay inside these ranges and needn't reach their ends.
All inputs are finite; a program needn't handle non-finite values.
Results may differ from the reference program's by a relative error of at most 0.03.
Values may be sent and summed in bfloat16 or wider, within the bound.
No kernel may reach another device: no remote copies, remote signals or barrier semaphores. Data moves between devices by JAX's collectives and lax.ppermute only.
A program may use at most 256 MiB of HBM per device.

```python
import jax
import jax.numpy as jnp
from jax import lax

D = 1152
HEADS = 16
HEAD_DIM = 72
FF = 4608
FRAMES = 16
PLACES = 256
CLIPS = 1
FRAME_ROWS = 16
PLACE_BLOCK = 128
N_TENSOR = 2


def shard_levels(stream_key, shape, split, low, high):
    level = 1.0
    for axis_at, parts in split:
        heights = jax.random.uniform(jax.random.fold_in(jax.random.fold_in(stream_key, 6), axis_at), (parts,), jnp.float32, low / len(split), high / len(split))
        level = level * jnp.repeat(jnp.exp(heights), shape[axis_at] // parts).reshape((-1,) + (1,) * (len(shape) - 1 - axis_at))
    return level


def noise(rng, shape, scale, most, shards=(), held_as=jnp.bfloat16):
    loudness = shard_levels(rng, shape, shards, -0.22, 0.18) if shards else 1.0
    drawn = jax.random.normal(rng, shape, jnp.float32) * scale * loudness
    return jnp.minimum(jnp.maximum(drawn, -most), most).astype(held_as)


def setup_inputs(seed: int = 0) -> dict:
    splits = jax.random.split(jax.random.key(seed), 12)
    return {
        "tokens": noise(splits[0], (FRAME_ROWS, N_TENSOR, PLACE_BLOCK, D), 1.0, 6.0, ((0, 16), (1, 2))),
        "cond": noise(splits[1], (CLIPS, D), 1.0, 6.0),
        "out_grad": noise(splits[2], (FRAME_ROWS, N_TENSOR, PLACE_BLOCK, D), 1.0, 6.0, ((1, 2), (2, 16))),
        "w_qkv": noise(splits[3], (2, D, 3, D), D ** -0.5, 0.1875, ((1, 16), (3, 2))),
        "w_out": noise(splits[4], (2, D, D), (D // 16) ** -0.5, 0.75, ((1, 2), (2, 16))),
        "w_fc1": noise(splits[5], (2, D, FF), D ** -0.5, 0.1875, ((1, 16), (2, 2))),
        "w_fc2": noise(splits[6], (2, FF, D), (FF // 2) ** -0.5, 0.125, ((1, 2), (2, 16))),
        "w_ada": noise(splits[7], (2, D, 6, D), D ** -0.5, 0.1875, ((1, 32),)),
        "b_ada": noise(splits[8], (2, 6, D), 0.5, 3.0, ((2, 32),)),
        "b_proj": noise(splits[9], (2, 4, D), 0.5, 3.0, ((2, 32),)),
        "b_fc1": noise(splits[10], (2, FF), 0.5, 3.0, ((1, 32),)),
    }


epsilon = 1e-06
highest = lax.Precision.HIGHEST

@jax.custom_vjp
def low(v):
    return lax.optimization_barrier(v.astype(jnp.bfloat16)).astype(jnp.float32)

@jax.custom_vjp
def low_back(v):
    return v

def low_keep(v):
    return (low(v), None)

def low_pass(kept, grad):
    return (grad,)

def back_keep(v):
    return (v, None)

def back_low(kept, grad):
    return (low(grad),)
low.defvjp(low_keep, low_pass)
low_back.defvjp(back_keep, back_low)

def matmul(left_side, right_side):
    return jnp.dot(left_side, right_side, precision=highest)

def normalize(values):
    average = lax.optimization_barrier(jnp.mean(values, axis=-1, keepdims=True))
    centred = values - average
    variance = lax.optimization_barrier(jnp.mean(centred * centred, axis=-1, keepdims=True))
    return centred * lax.rsqrt(variance + epsilon)

def attention(query_heads, keys_heads, values_heads):
    score_scale = HEAD_DIM ** (-0.5)
    scores = low_back(jnp.einsum('glhe,gmhe->ghlm', query_heads, keys_heads, precision=highest) * score_scale)
    weights = jax.nn.softmax(scores, axis=-1)
    return jnp.einsum('ghlm,gmhe->glhe', low(weights), values_heads, precision=highest)

def block(current, modulation, wqkv, wout, wfc1, wfc2, bproj, bfc1, across_frames):
    hidden_attn = low(normalize(current) * (1.0 + modulation[1]) + modulation[0])
    flat_rows = hidden_attn.reshape(FRAMES * PLACES, D)
    query_rows = low_back(low(matmul(flat_rows, wqkv[:, 0]) + bproj[0]))
    keys_rows = low_back(low(matmul(flat_rows, wqkv[:, 1])))
    value_rows = low_back(low(matmul(flat_rows, wqkv[:, 2]) + bproj[1]))

    def split_heads(values):
        shaped = values.reshape(FRAMES, PLACES, HEADS, HEAD_DIM)
        if across_frames:
            shaped = shaped.transpose(1, 0, 2, 3)
        return shaped
    attended = attention(split_heads(query_rows), split_heads(keys_rows), split_heads(value_rows))
    if across_frames:
        attended = attended.transpose(1, 0, 2, 3)
    attended = low_back(low(attended.reshape(FRAMES * PLACES, D)))
    branch_attn = low_back(matmul(attended, wout) + bproj[2])
    middle = current + modulation[2] * branch_attn.reshape(FRAMES, PLACES, D)
    hidden_mlp = low(normalize(middle) * (1.0 + modulation[4]) + modulation[3]).reshape(FRAMES * PLACES, D)
    inner_pre = low_back(matmul(hidden_mlp, wfc1) + bfc1)
    activated = low(jax.nn.gelu(inner_pre, approximate=True))
    branch_mlp = low_back(matmul(activated, wfc2) + bproj[3])
    return middle + modulation[5] * branch_mlp.reshape(FRAMES, PLACES, D)

def forward(clip_tokens, clip_cond, w_qkv, w_out, w_fc1, w_fc2, w_ada, b_ada, b_proj, b_fc1):
    current = clip_tokens.reshape(FRAMES, PLACES, D)
    gated_cond = low(jax.nn.silu(clip_cond))
    for layer_index in range(2):
        modulation = matmul(gated_cond[None, :], w_ada[layer_index].reshape(D, 6 * D)).reshape(6, D) + b_ada[layer_index]
        current = block(current, modulation, w_qkv[layer_index], w_out[layer_index], w_fc1[layer_index], w_fc2[layer_index], b_proj[layer_index], b_fc1[layer_index], layer_index == 1)
        if layer_index == 0:
            current = low_back(low(current))
    return current.reshape(FRAMES, N_TENSOR, PLACE_BLOCK, D)

def reference(tokens, cond, out_grad, w_qkv, w_out, w_fc1, w_fc2, w_ada, b_ada, b_proj, b_fc1):
    params = tuple((array_item.astype(jnp.float32) for array_item in (w_qkv, w_out, w_fc1, w_fc2, w_ada, b_ada, b_proj, b_fc1)))
    clip_shape = (CLIPS, FRAMES, N_TENSOR, PLACE_BLOCK, D)
    clip_tokens = tokens.astype(jnp.float32).reshape(clip_shape)
    clip_cots = out_grad.astype(jnp.float32).reshape(clip_shape)
    cond_float = cond.astype(jnp.float32)

    def per_clip(totals, inputs):
        one_tokens, one_cond, one_cot = inputs
        result, pullback = jax.vjp(forward, one_tokens, one_cond, *params)
        gradients = pullback(one_cot)
        totals = tuple((running + added for running, added in zip(totals, gradients[2:])))
        return (totals, (result.astype(jnp.bfloat16), gradients[0], gradients[1]))
    initial = tuple((jnp.zeros_like(array_item) for array_item in params))
    totals, (outputs, token_grads, cond_grads) = lax.scan(per_clip, initial, (clip_tokens, cond_float, clip_cots))
    row_shape = (FRAME_ROWS, N_TENSOR, PLACE_BLOCK, D)
    return (outputs.reshape(row_shape), token_grads.reshape(row_shape), cond_grads, totals[0], totals[1], totals[2], totals[3], totals[4], totals[5], totals[6], totals[7])
```

```python
import functools

import jax
import jax.numpy as jnp
from jax import lax
from jax.experimental import pallas as pl
from jax.experimental.pallas import tpu as pltpu
from jax.sharding import PartitionSpec as P

HEAD_DIM = 72
FRAMES = 16


epsilon = 1e-06
highest = lax.Precision.HIGHEST
low = jnp.bfloat16
wide = jnp.float32
everyone = ("dp", "tensor")


def normalize(values):
    average = jnp.mean(values, axis=-1, keepdims=True)
    centred = values - average
    inverse = lax.rsqrt(jnp.mean(centred * centred, axis=-1, keepdims=True) + epsilon)
    return (centred * inverse, inverse)


def normalize_back(normed, inverse, upstream):
    first_moment = jnp.mean(upstream, axis=-1, keepdims=True)
    second_moment = jnp.mean(upstream * normed, axis=-1, keepdims=True)
    return inverse * (upstream - first_moment - normed * second_moment)


def product(left_side, right_side):
    return jnp.dot(left_side, right_side, preferred_element_type=wide)


def product_left(left_side, right_side):
    return lax.dot_general(
        left_side, right_side, (((0,), (0,)), ((), ())), preferred_element_type=wide
    )


def product_right(left_side, right_side):
    return lax.dot_general(
        left_side, right_side, (((1,), (1,)), ((), ())), preferred_element_type=wide
    )


def gelu_tanh(values):
    return jax.nn.gelu(values, approximate=True)


def bit_orders(count):
    bits = list(range(count.bit_length() - 1))
    tail, head = bits[:2], bits[2:]
    return (head + tail, head + tail[::-1])


def swap_bit(values, bit, count):
    return lax.ppermute(values, "dp", [(i, i ^ (1 << bit)) for i in range(count)])


def my_bit(bit):
    return (lax.axis_index("dp") >> bit) & 1


def gather_rows(shard, order, count):
    rows, columns = shard.shape
    held = shard[None]
    done = []
    for bit in order:
        got = swap_bit(held, bit, count)
        below = 1 << len([other for other in done if other < bit])
        shape = (-1, below, rows, columns)
        mine, theirs = held.reshape(shape), got.reshape(shape)
        first = my_bit(bit) == 0
        held = jnp.stack(
            [jnp.where(first, mine, theirs), jnp.where(first, theirs, mine)], axis=1
        ).reshape(-1, rows, columns)
        done.append(bit)
    return held.reshape(-1, columns)


def scatter_rows(partial, order, count):
    rows, columns = partial.shape[0] // count, partial.shape[1]
    held = partial.reshape(count, rows, columns)
    left = list(order)
    for bit in order[::-1]:
        left.remove(bit)
        below = 1 << len([other for other in left if other < bit])
        split = held.reshape(-1, 2, below, rows, columns)
        side = my_bit(bit)
        keep = lax.dynamic_index_in_dim(split, side, 1, keepdims=False)
        send = lax.dynamic_index_in_dim(split, 1 - side, 1, keepdims=False)
        got = swap_bit(send.astype(low), bit, count)
        held = keep.astype(wide) + got.astype(wide)
        if left:
            held = held.astype(low)
    return held.reshape(rows, columns)


def swap_tensor(values):
    return lax.ppermute(values, "tensor", [(0, 1), (1, 0)])


def add_halves(partial):
    mine = partial.astype(low)
    return mine.astype(wide) + swap_tensor(mine).astype(wide)


def both_halves(values):
    return lax.all_gather(values, "tensor", axis=1, tiled=True)


def own_half(values):
    return lax.dynamic_slice_in_dim(
        values, lax.axis_index("tensor") * (values.shape[1] // 2), values.shape[1] // 2, 1
    )


def deal(values):
    return lax.all_to_all(values, everyone, split_axis=0, concat_axis=0, tiled=True)


def sum_to_owner(values, owners):
    lead = values.shape[:-1]
    dealt = jnp.moveaxis(values.reshape(lead + (owners, -1)), -2, 0)
    return dealt.reshape(owners, -1)


def from_owners(values, lead):
    owners = values.shape[0]
    return jnp.moveaxis(values.reshape((owners,) + lead + (-1,)), 0, -2).reshape(lead + (-1,))


def same_group(rows, place_count, across):
    first = lax.broadcasted_iota(jnp.int32, (rows, rows), 0)
    second = lax.broadcasted_iota(jnp.int32, (rows, rows), 1)
    if across:
        period = FRAMES * place_count
        alike = lax.rem(first, place_count) == lax.rem(second, place_count)
        if rows > period:
            alike = alike & (lax.div(first, period) == lax.div(second, period))
        return alike
    if rows == place_count:
        return None
    return lax.div(first, place_count) == lax.div(second, place_count)


def head_probs(query, keys, mask):
    scores = product_right(query, keys) * (HEAD_DIM ** (-0.5))
    if mask is not None:
        scores = jnp.where(mask, scores, -1e30)
    exponent = jnp.exp(scores - jnp.max(scores, axis=-1, keepdims=True))
    return exponent / jnp.sum(exponent, axis=-1, keepdims=True)


def attend_kernel(place_count, across, joined_ref, out_ref):
    rows, width = out_ref.shape
    mask = same_group(rows, place_count, across)
    for start in range(0, width, HEAD_DIM):
        query, keys, value = (
            joined_ref[:, part * width + start : part * width + start + HEAD_DIM]
            for part in range(3)
        )
        probs = head_probs(query, keys, mask).astype(low)
        out_ref[:, start : start + HEAD_DIM] = product(probs, value).astype(low)


def attend_back_kernel(place_count, across, joined_ref, upstream_ref, out_ref):
    rows, width = upstream_ref.shape
    mask = same_group(rows, place_count, across)
    score_scale = HEAD_DIM ** (-0.5)
    for start in range(0, width, HEAD_DIM):
        query, keys, value = (
            joined_ref[:, part * width + start : part * width + start + HEAD_DIM]
            for part in range(3)
        )
        upstream = upstream_ref[:, start : start + HEAD_DIM]
        probs = head_probs(query, keys, mask)
        value_grad = product_left(probs.astype(low), upstream)
        prob_grad = product_right(upstream, value)
        centre = jnp.sum(probs * prob_grad, axis=-1, keepdims=True)
        score_grad = (probs * (prob_grad - centre)).astype(low)
        query_grad = product(score_grad, keys) * score_scale
        keys_grad = product_left(score_grad, query) * score_scale
        for part, grad in enumerate((query_grad, keys_grad, value_grad)):
            out_ref[:, part * width + start : part * width + start + HEAD_DIM] = grad.astype(low)


def attend(joined, place_count, across):
    rows, width = joined.shape[0], joined.shape[1] // 3
    heads = width // HEAD_DIM
    return pl.pallas_call(
        functools.partial(attend_kernel, place_count, across),
        out_shape=jax.ShapeDtypeStruct((rows, width), low),
        name="attend",
        cost_estimate=pl.CostEstimate(
            flops=4 * heads * rows * rows * HEAD_DIM,
            bytes_accessed=8 * rows * width,
            transcendentals=heads * rows * rows,
        ),
    )(joined)


def attend_back(joined, upstream, place_count, across):
    rows, width = upstream.shape
    heads = width // HEAD_DIM
    return pl.pallas_call(
        functools.partial(attend_back_kernel, place_count, across),
        out_shape=jax.ShapeDtypeStruct((rows, 3 * width), low),
        name="attend_back",
        cost_estimate=pl.CostEstimate(
            flops=10 * heads * rows * rows * HEAD_DIM,
            bytes_accessed=14 * rows * width,
            transcendentals=heads * rows * rows,
        ),
    )(joined, upstream)


def block_forward(inputs, modulation, weights, biases, across):
    wattn, wfc1, wfc2 = weights
    bias_joined, bias_out, bias_fc2, bias_fc1 = biases
    mod_parts = [modulation[:, index][:, None, :] for index in range(6)]
    shape = inputs.shape
    rows, width = shape[0] * shape[1], shape[2]
    joined_width = bias_joined.shape[0]
    normed_attn, inverse_attn = normalize(inputs)
    hidden_attn = (normed_attn * (1.0 + mod_parts[1]) + mod_parts[0]).astype(low)
    flat_attn = hidden_attn.reshape(rows, width)
    joined = (product(flat_attn, wattn[:, :joined_width]) + bias_joined).astype(low)
    attended = attend(joined, shape[1], across)
    branch_attn = (
        add_halves(product_right(attended, wattn[:, joined_width:])) + bias_out
    ).reshape(shape)
    middle = inputs + mod_parts[2] * branch_attn
    normed_mlp, inverse_mlp = normalize(middle)
    hidden_mlp = (normed_mlp * (1.0 + mod_parts[4]) + mod_parts[3]).astype(low)
    flat_mlp = hidden_mlp.reshape(rows, width)
    inner_pre = product(flat_mlp, wfc1) + bias_fc1
    activated = gelu_tanh(inner_pre).astype(low)
    branch_mlp = (add_halves(product_right(activated, wfc2)) + bias_fc2).reshape(shape)
    result = middle + mod_parts[5] * branch_mlp
    saved = (
        normed_attn,
        inverse_attn,
        flat_attn,
        joined,
        attended,
        branch_attn,
        normed_mlp,
        inverse_mlp,
        flat_mlp,
        inner_pre,
        activated,
        branch_mlp,
    )
    return (result, saved)


def block_backward(upstream, saved, modulation, weights, across, scatter):
    (
        normed_attn,
        inverse_attn,
        flat_attn,
        joined,
        attended,
        branch_attn,
        normed_mlp,
        inverse_mlp,
        flat_mlp,
        inner_pre,
        activated,
        branch_mlp,
    ) = saved
    wattn, wfc1, wfc2 = weights
    mod_parts = [modulation[:, index][:, None, :] for index in range(6)]
    shape = upstream.shape
    rows, width = flat_attn.shape
    joined_width = joined.shape[1]
    part_width = joined_width // 3
    gate_mlp_grad = jnp.sum(upstream * branch_mlp, axis=1)
    mlp_out_grad = (upstream * mod_parts[5]).astype(low)
    fc2_bias_grad = jnp.sum(mlp_out_grad.astype(wide), axis=(0, 1))
    flat_out_grad = mlp_out_grad.reshape(rows, width)
    fc2_reduced = scatter(product_left(flat_out_grad, activated).astype(low), 1)
    activated_grad = product(flat_out_grad, wfc2)
    inner_grad = jax.vjp(gelu_tanh, inner_pre)[1](activated_grad)[0].astype(low)
    fc1_bias_local = jnp.sum(inner_grad.astype(wide), axis=0)
    fc1_reduced = scatter(product_left(flat_mlp, inner_grad).astype(low), 0)
    hidden_mlp_grad = add_halves(product_right(inner_grad, wfc1)).reshape(shape)
    scale_mlp_grad = jnp.sum(hidden_mlp_grad * normed_mlp, axis=1)
    shift_mlp_grad = jnp.sum(hidden_mlp_grad, axis=1)
    middle_grad = upstream + normalize_back(
        normed_mlp, inverse_mlp, hidden_mlp_grad * (1.0 + mod_parts[4])
    )
    gate_attn_grad = jnp.sum(middle_grad * branch_attn, axis=1)
    attn_out_grad = (middle_grad * mod_parts[2]).astype(low)
    out_bias_grad = jnp.sum(attn_out_grad.astype(wide), axis=(0, 1))
    flat_attn_grad = attn_out_grad.reshape(rows, width)
    out_weight_grad = product_left(flat_attn_grad, attended).astype(low)
    attended_grad = product(flat_attn_grad, wattn[:, joined_width:]).astype(low)
    joined_grad = attend_back(joined, attended_grad, shape[1], across)
    joined_weight_grad = product_left(flat_attn, joined_grad).astype(low)
    attn_reduced = scatter(jnp.concatenate([joined_weight_grad, out_weight_grad], axis=1), 0)
    hidden_attn_grad = add_halves(product_right(joined_grad, wattn[:, :joined_width])).reshape(
        shape
    )
    scale_attn_grad = jnp.sum(hidden_attn_grad * normed_attn, axis=1)
    shift_attn_grad = jnp.sum(hidden_attn_grad, axis=1)
    input_grad = middle_grad + normalize_back(
        normed_attn, inverse_attn, hidden_attn_grad * (1.0 + mod_parts[1])
    )
    mod_grad = jnp.stack(
        [
            shift_attn_grad,
            scale_attn_grad,
            gate_attn_grad,
            shift_mlp_grad,
            scale_mlp_grad,
            gate_mlp_grad,
        ],
        axis=1,
    )
    joined_bias = jnp.sum(joined_grad.astype(wide), axis=0)
    proj_grad = jnp.stack(
        [
            widen(joined_bias[:part_width]),
            widen(joined_bias[2 * part_width :]),
            0.5 * out_bias_grad,
            0.5 * fc2_bias_grad,
        ]
    )
    hidden_grad = widen(fc1_bias_local)
    return (input_grad, 0.5 * mod_grad, (attn_reduced, fc1_reduced, fc2_reduced), proj_grad, hidden_grad)


def widen(local_part):
    offset = lax.axis_index("tensor") * local_part.shape[0]
    return lax.dynamic_update_slice_in_dim(
        jnp.zeros((local_part.shape[0] * 2,), wide), local_part, offset, 0
    )


def tensor_part(values):
    part = values.shape[-1] // 2
    return lax.dynamic_slice_in_dim(
        values, lax.axis_index("tensor") * part, part, values.ndim - 1
    )


def per_device(tokens, cond, out_grad, w_qkv, w_out, w_fc1, w_fc2, w_ada, b_ada, b_proj, b_fc1):
    dp_count = lax.axis_size("dp")
    all_devices = lax.axis_size(everyone)
    flat_index = lax.axis_index(everyone)
    width = tokens.shape[3]
    clip_count = cond.shape[0]
    own_rows, head_width = w_qkv.shape[1], w_qkv.shape[3]
    own_width = width // all_devices
    own_start = flat_index * own_width
    orders = bit_orders(dp_count)

    gathered = []
    for layer in range(2):
        shards = (
            jnp.concatenate([w_qkv[layer].reshape(own_rows, 3 * head_width), w_out[layer].T], axis=1),
            w_fc1[layer],
            w_fc2[layer].T,
        )
        gathered.append(
            [
                gather_rows(shard, orders[(index + layer) % 2], dp_count)
                for index, shard in enumerate(shards)
            ]
        )

    cond_float = cond.astype(wide)
    gated_low = jax.nn.silu(cond_float).astype(low)
    gated_own = lax.dynamic_slice_in_dim(gated_low, own_start, own_width, 1)
    partial_mod = jnp.einsum("cd,ldkj->lckj", gated_own, w_ada, preferred_element_type=wide)
    own_mod = jnp.sum(deal(sum_to_owner(partial_mod, all_devices)), axis=0).reshape(
        2, clip_count, 6, own_width
    )
    own_mod = own_mod + b_ada.astype(wide)[:, None]
    pieces = (own_mod, b_proj.astype(wide), b_fc1.astype(wide))
    packed = jnp.concatenate([piece.reshape(-1) for piece in pieces])
    dealt = deal(jnp.broadcast_to(packed[None], (all_devices, packed.shape[0])))
    first_end, second_end = pieces[0].size, pieces[0].size + pieces[1].size
    modulation = from_owners(dealt[:, :first_end], (2, clip_count, 6))
    proj_full = from_owners(dealt[:, first_end:second_end], (2, 4))
    hidden_full = from_owners(dealt[:, second_end:], (2,))

    frames_dev = tokens.shape[0]
    frame_ids = lax.axis_index("dp") * frames_dev + jnp.arange(frames_dev, dtype=jnp.int32)
    onehot = (
        frame_ids[:, None] // FRAMES == jnp.arange(clip_count, dtype=jnp.int32)[None, :]
    ).astype(wide)
    first_mod = jnp.einsum("gc,ckd->gkd", onehot, modulation[0], precision=highest)
    second_mod = jnp.repeat(modulation[1], FRAMES, axis=0)

    def layer_biases(layer):
        bias_query = tensor_part(proj_full[layer, 0])
        bias_value = tensor_part(proj_full[layer, 1])
        return (
            jnp.concatenate([bias_query, jnp.zeros_like(bias_query), bias_value]),
            proj_full[layer, 2],
            proj_full[layer, 3],
            tensor_part(hidden_full[layer]),
        )

    def merge(values):
        return values.reshape(values.shape[0], -1, width)

    first_in = merge(both_halves(tokens)).astype(wide)
    first_biases, second_biases = layer_biases(0), layer_biases(1)
    first_out, first_saved = block_forward(first_in, first_mod, gathered[0], first_biases, False)
    sent = own_half(first_out.astype(low))[:, None]
    arrived = lax.all_to_all(sent, "dp", split_axis=2, concat_axis=0, tiled=True)
    second_in = merge(both_halves(arrived)).astype(wide)
    second_out, second_saved = block_forward(
        second_in, second_mod, gathered[1], second_biases, True
    )
    output = own_half(second_out.astype(low))[:, None]

    def scatter(layer):
        return lambda partial, which: scatter_rows(partial, orders[(which + layer) % 2], dp_count)

    second_upstream = merge(both_halves(out_grad)).astype(wide)
    second_grad, second_dmod, second_reduced, second_proj, second_hidden = block_backward(
        second_upstream, second_saved, second_mod, gathered[1], True, scatter(1)
    )
    sent_back = own_half(second_grad.astype(low))[:, None]
    arrived_back = lax.all_to_all(sent_back, "dp", split_axis=0, concat_axis=2, tiled=True)
    first_upstream = merge(both_halves(arrived_back)).astype(wide)
    first_grad, first_dmod, first_reduced, first_proj, first_hidden = block_backward(
        first_upstream, first_saved, first_mod, gathered[0], False, scatter(0)
    )
    tokens_grad = own_half(first_grad)[:, None]

    dmod_clips = jnp.stack(
        [
            jnp.einsum("gc,gkd->ckd", onehot, first_dmod, precision=highest),
            jnp.sum(second_dmod.reshape(clip_count, FRAMES, 6, width), axis=1),
        ]
    )
    small = (
        dmod_clips,
        jnp.stack([first_proj, second_proj]),
        jnp.stack([first_hidden, second_hidden]),
    )
    owned = jnp.sum(
        deal(jnp.concatenate([sum_to_owner(piece, all_devices) for piece in small], axis=1)), axis=0
    )
    own_dmod = owned[:first_end]
    b_proj_grad = owned[first_end:second_end].reshape(2, 4, own_width)
    b_fc1_grad = owned[second_end:].reshape(2, -1)
    summed_mod = from_owners(
        deal(jnp.broadcast_to(own_dmod[None], (all_devices, own_dmod.shape[0]))), (2, clip_count, 6)
    )
    w_ada_grad = jnp.einsum(
        "cd,lckj->ldkj", gated_own.astype(wide), summed_mod, precision=highest
    )
    b_ada_grad = jnp.sum(own_dmod.reshape(2, clip_count, 6, own_width), axis=1)
    silu_grad = jnp.einsum("lckj,ldkj->cd", summed_mod, w_ada.astype(wide), precision=highest)
    cond_own = lax.dynamic_slice_in_dim(cond_float, own_start, own_width, 1)
    cond_grad = jax.vjp(jax.nn.silu, cond_own)[1](silu_grad)[0]

    reduced = (first_reduced, second_reduced)
    joined_width = 3 * head_width
    w_qkv_grad = jnp.stack(
        [part[0][:, :joined_width].reshape(own_rows, 3, head_width) for part in reduced]
    )
    w_out_grad = jnp.stack([part[0][:, joined_width:].T for part in reduced])
    w_fc1_grad = jnp.stack([part[1] for part in reduced])
    w_fc2_grad = jnp.stack([part[2].T for part in reduced])
    return (
        output,
        tokens_grad,
        cond_grad,
        w_qkv_grad,
        w_out_grad,
        w_fc1_grad,
        w_fc2_grad,
        w_ada_grad,
        b_ada_grad,
        b_proj_grad,
        b_fc1_grad,
    )


def solution(mesh):
    return jax.shard_map(
        per_device,
        mesh=mesh,
        in_specs=(
            P("dp", "tensor", None, None),
            P(),
            P(None, "tensor", "dp", None),
            P(None, "dp", None, "tensor"),
            P(None, "tensor", "dp"),
            P(None, "dp", "tensor"),
            P(None, "tensor", "dp"),
            P(None, ("dp", "tensor"), None, None),
            P(None, None, ("dp", "tensor")),
            P(None, None, ("dp", "tensor")),
            P(None, ("dp", "tensor")),
        ),
        out_specs=(
            P(None, "tensor", "dp", None),
            P("dp", "tensor", None, None),
            P(None, ("dp", "tensor")),
            P(None, "dp", None, "tensor"),
            P(None, "tensor", "dp"),
            P(None, "dp", "tensor"),
            P(None, "tensor", "dp"),
            P(None, ("dp", "tensor"), None, None),
            P(None, None, ("dp", "tensor")),
            P(None, None, ("dp", "tensor")),
            P(None, ("dp", "tensor")),
        ),
        check_vma=False,
    )
```

```python
import functools

import jax
import jax.numpy as jnp
from jax import lax
from jax.experimental import pallas as pl
from jax.experimental.pallas import tpu as pltpu
from jax.sharding import PartitionSpec as P

HEAD_DIM = 72
FRAMES = 16


epsilon = 1e-06
highest = lax.Precision.HIGHEST
low = jnp.bfloat16
wide = jnp.float32
everyone = ("dp", "tensor")


def layer_norm(values):
    centred = values - jnp.mean(values, axis=-1, keepdims=True)
    inverse = lax.rsqrt(jnp.mean(centred * centred, axis=-1, keepdims=True) + epsilon)
    return (centred * inverse, inverse)


def layer_norm_back(normed, inverse, upstream):
    first_moment = jnp.mean(upstream, axis=-1, keepdims=True)
    second_moment = jnp.mean(upstream * normed, axis=-1, keepdims=True)
    return inverse * (upstream - first_moment - normed * second_moment)


def product(left_side, right_side):
    return jnp.dot(left_side, right_side, preferred_element_type=wide)


def product_left(left_side, right_side):
    return lax.dot_general(
        left_side, right_side, (((0,), (0,)), ((), ())), preferred_element_type=wide
    )


def product_right(left_side, right_side):
    return lax.dot_general(
        left_side, right_side, (((1,), (1,)), ((), ())), preferred_element_type=wide
    )


PLANE = 2
PAIR = 2


def swap_bit(values, bit, count):
    return lax.ppermute(values, "dp", [(i, i ^ (1 << bit)) for i in range(count)])


def my_bit(bit):
    return (lax.axis_index("dp") >> bit) & 1


def after(value, *others):
    return lax.optimization_barrier((value,) + others)[0]


def outer_bits(count):
    return range(PLANE, count.bit_length() - 1)


def pick(first, mine, theirs, axis):
    return jnp.stack(
        [jnp.where(first, mine, theirs), jnp.where(first, theirs, mine)], axis=axis
    )


def gather_outer(shard, count):
    paired = isinstance(shard, tuple)
    rows, columns = shard[0].shape if paired else shard.shape
    held = shard[0][None] if paired else shard[None]
    for bit in outer_bits(count):
        sent = shard[1][None] if bit == PAIR and paired else held
        got = swap_bit(sent, bit, count)
        held = pick(my_bit(bit) == 0, held, got, 0).reshape(-1, rows, columns)
    return held


def arrange_kernel(me_ref, own_ref, across_ref, along_ref, low_ref, high_ref, out_ref):
    me = me_ref[0]
    out_ref[me] = own_ref[0]
    out_ref[me ^ 1] = across_ref[0]
    out_ref[me ^ 2] = along_ref[0]
    in_low = pl.program_id(0) < pl.num_programs(0) // 2

    @pl.when(in_low)
    def _():
        out_ref[me ^ 3] = low_ref[0]

    @pl.when(jnp.logical_not(in_low))
    def _():
        out_ref[me ^ 3] = high_ref[0]


def arrange(own, across, along, low_part, high_part):
    groups, rows, columns = own.shape
    half = groups // 2
    block = (1, rows, columns)
    whole = pl.BlockSpec(block, lambda i, me: (i, 0, 0))
    me = jnp.reshape(lax.axis_index("dp") & 3, (1,)).astype(jnp.int32)
    out = pl.pallas_call(
        arrange_kernel,
        out_shape=jax.ShapeDtypeStruct((groups * 4, rows, columns), own.dtype),
        grid_spec=pltpu.PrefetchScalarGridSpec(
            num_scalar_prefetch=1,
            grid=(groups,),
            in_specs=[
                whole,
                whole,
                whole,
                pl.BlockSpec(block, lambda i, me: (jnp.minimum(i, half - 1), 0, 0)),
                pl.BlockSpec(block, lambda i, me: (jnp.maximum(i - half, 0), 0, 0)),
            ],
            out_specs=pl.BlockSpec((4, rows, columns), lambda i, me: (i, 0, 0)),
        ),
        name="arrange",
        cost_estimate=pl.CostEstimate(
            flops=0, bytes_accessed=16 * groups * rows * columns, transcendentals=0
        ),
    )(me, own, across, along, low_part, high_part)
    return out.reshape(groups * 4 * rows, columns)


def gather_all(shards, count):
    full = []
    last_outer = last_plane = None
    for shard in shards:
        if last_outer is not None:
            shard = lax.optimization_barrier((shard, last_outer))[0]
        own = gather_outer(shard, count)
        last_outer = own
        if last_plane is not None:
            own = after(own, *last_plane)
        across, along = swap_bit(own, 0, count), swap_bit(own, 1, count)
        last_plane = (across, along)
        half = own.shape[0] // 2
        low_part = swap_bit(across[:half], 1, count)
        high_part = swap_bit(along[half:], 0, count)
        full.append(arrange(own, across, along, low_part, high_part))
    return full


def place_scalars():
    return jnp.stack([lax.axis_index("tensor"), lax.axis_index("dp") & 3]).astype(jnp.int32)


def weight_grad_kernel(count, starts, place_ref, *refs):
    pairs = len(starts)
    operands, outs, total = refs[: 2 * pairs], refs[2 * pairs : -1], refs[-1]
    me = place_ref[1]
    rows = total.shape[0] // count
    for index, start in enumerate(starts):
        left, right = operands[2 * index], operands[2 * index + 1]
        total[:, start : start + right.shape[1]] = product_left(left[...], right[...])
        spare = -right.shape[1] % 128
        if spare:
            end = start + right.shape[1]
            total[:, end : end + spare] = jnp.zeros((total.shape[0], spare), wide)
    for relative, out in enumerate(outs):
        mate = me ^ relative
        if rows % 8 == 0:

            @pl.loop(0, count // 4)
            def _(group, mate=mate, out=out):
                first = pl.multiple_of((group * 4 + mate) * rows, 8)
                out[group] = total[pl.ds(first, rows), :].astype(low)
        else:
            for place in range(4):

                @pl.when(mate == place)
                def _(place=place, out=out):
                    for group in range(count // 4):
                        first = (group * 4 + place) * rows
                        out[group] = total[first : first + rows, :].astype(low)


def scatter_product(pairs, paired):
    count = lax.axis_size("dp")
    groups = count // 4
    half = groups // 2
    width = pairs[0][0].shape[1]
    rows = width // count
    starts, columns = [], 0
    for _, right in pairs:
        starts.append(columns)
        columns += padded(right.shape[1])
    tokens = pairs[0][0].shape[0]
    own, across, along, far = pl.pallas_call(
        functools.partial(weight_grad_kernel, count, tuple(starts)),
        out_shape=[jax.ShapeDtypeStruct((groups, rows, columns), low)] * 4,
        in_specs=[pl.BlockSpec(memory_space=pltpu.SMEM)]
        + [pl.BlockSpec(memory_space=pltpu.VMEM)] * (2 * len(pairs)),
        scratch_shapes=[pltpu.VMEM((width, columns), wide)],
        name="weight_grad",
        cost_estimate=pl.CostEstimate(
            flops=2 * tokens * width * columns,
            bytes_accessed=2 * width * columns + 4 * tokens * (width + columns),
            transcendentals=0,
        ),
    )(place_scalars(), *[operand for pair in pairs for operand in pair])
    low_part = swap_bit(far[:half], 1, count)
    high_part = swap_bit(far[half:], 0, count)
    across = jnp.concatenate(
        [(across[:half].astype(wide) + low_part.astype(wide)).astype(low), across[half:]]
    )
    along = jnp.concatenate(
        [along[:half], (along[half:].astype(wide) + high_part.astype(wide)).astype(low)]
    )
    got_across, got_along = swap_bit(across, 0, count), swap_bit(along, 1, count)
    held = own.astype(wide) + got_across.astype(wide) + got_along.astype(wide)
    for bit in reversed(outer_bits(count)):
        split = held.reshape(2, -1, rows, columns)
        side = my_bit(bit)
        keep = lax.dynamic_index_in_dim(split, side, 0, keepdims=False)
        send = lax.dynamic_index_in_dim(split, 1 - side, 0, keepdims=False)
        got = swap_bit(send.astype(low), bit, count).astype(wide)
        if bit == PAIR and paired:
            return pick(side == 0, keep[0], got[0], 0)
        held = keep + got
    return held[0]


def swap_tensor(values):
    return lax.ppermute(values, "tensor", [(0, 1), (1, 0)])


def both_halves(values):
    return lax.all_gather(values, "tensor", axis=1, tiled=True)


def own_half(values):
    return lax.dynamic_slice_in_dim(
        values, lax.axis_index("tensor") * (values.shape[1] // 2), values.shape[1] // 2, 1
    )


def rows_half(values, axis):
    half = values.shape[axis] // 2
    return values.reshape(values.shape[:axis] + (2, half) + values.shape[axis + 1 :])


def pair_rows(values):
    tensor = lax.axis_index("tensor")
    half = lax.dynamic_index_in_dim(rows_half(values, 0), tensor, 0, keepdims=False)
    got = swap_bit(half, PAIR, lax.axis_size("dp"))
    return jnp.concatenate([values, lax.all_gather(got, "tensor", axis=0, tiled=True)])


def pair_sum(keep, send):
    chip = keep.astype(wide) + swap_tensor(send).astype(wide)
    got = swap_bit(chip[1].astype(low), PAIR, lax.axis_size("dp"))
    total = (chip[0] + got.astype(wide)).astype(low)
    return lax.all_gather(total, "tensor", axis=0, tiled=True)


def unit_start(units):
    return (lax.axis_index("tensor") * 2 + my_bit(PAIR)) * units


def deal(values):
    return lax.all_to_all(values, everyone, split_axis=0, concat_axis=0, tiled=True)


def sum_to_owner(values, owners):
    lead = values.shape[:-1]
    dealt = jnp.moveaxis(values.reshape(lead + (owners, -1)), -2, 0)
    return dealt.reshape(owners, -1)


def from_owners(values, lead):
    owners = values.shape[0]
    return jnp.moveaxis(values.reshape((owners,) + lead + (-1,)), 0, -2).reshape(lead + (-1,))


def padded(width):
    return width + -width % 128


def fixed(*shape):
    return pl.BlockSpec(shape, lambda i, *_: (0,) * len(shape))


def by_rows(rows, *rest):
    return pl.BlockSpec((rows,) + rest, lambda i, *_: (i,) + (0,) * len(rest))


def cost(flops, bytes_accessed, transcendentals=0):
    return pl.CostEstimate(
        flops=flops, bytes_accessed=bytes_accessed, transcendentals=transcendentals
    )


def column_sum(values):
    return jnp.sum(values, axis=0, keepdims=True)


def same_place(rows, place_count):
    if rows == place_count:
        return None
    first = lax.broadcasted_iota(jnp.int32, (rows, rows), 0)
    second = lax.broadcasted_iota(jnp.int32, (rows, rows), 1)
    return lax.rem(first, place_count) == lax.rem(second, place_count)


def head_probs(query, keys, mask):
    scores = product_right(query, keys) * (HEAD_DIM ** (-0.5))
    if mask is not None:
        scores = jnp.where(mask, scores, -1e30)
    exponent = jnp.exp(scores - jnp.max(scores, axis=-1, keepdims=True))
    return exponent * (1.0 / jnp.sum(exponent, axis=-1, keepdims=True))


def attention_kernel(
    place_count, x_ref, mod_ref, weight_ref, bias_ref, hidden_ref, joined_ref, attended_ref, out_ref
):
    rows, width = attended_ref.shape
    joined_width = joined_ref.shape[1]
    normed, _ = layer_norm(x_ref[...].astype(wide))
    hidden = (normed * (1.0 + mod_ref[0, 1:2]) + mod_ref[0, 0:1]).astype(low)
    hidden_ref[...] = hidden
    joined_ref[...] = (product(hidden, weight_ref[:, :joined_width]) + bias_ref[...]).astype(low)
    mask = None if place_count is None else same_place(rows, place_count)
    for start in range(0, width, HEAD_DIM):
        query, keys, value = (
            joined_ref[:, part * width + start : part * width + start + HEAD_DIM]
            for part in range(3)
        )
        probs = head_probs(query, keys, mask).astype(low)
        attended_ref[:, start : start + HEAD_DIM] = product(probs, value).astype(low)
    out_ref[...] = product_right(
        attended_ref[...], weight_ref[:, joined_width : joined_width + width]
    ).astype(low)


def attention_back_kernel(
    place_count, upstream_ref, weight_ref, joined_ref, grad_ref, out_ref, bias_ref
):
    rows, joined_width = joined_ref.shape
    width = upstream_ref.shape[1] // 2
    score_scale = HEAD_DIM ** (-0.5)
    attended_grad = product(
        upstream_ref[...], weight_ref[:, joined_width : joined_width + width]
    ).astype(low)
    mask = None if place_count is None else same_place(rows, place_count)
    for start in range(0, width, HEAD_DIM):
        query, keys, value = (
            joined_ref[:, part * width + start : part * width + start + HEAD_DIM]
            for part in range(3)
        )
        upstream = attended_grad[:, start : start + HEAD_DIM]
        probs = head_probs(query, keys, mask)
        value_grad = product_left(probs.astype(low), upstream)
        prob_grad = product_right(upstream, value)
        centre = jnp.sum(probs * prob_grad, axis=-1, keepdims=True)
        score_grad = (probs * (prob_grad - centre)).astype(low)
        query_grad = product(score_grad, keys) * score_scale
        keys_grad = product_left(score_grad, query) * score_scale
        for part, grad in enumerate((query_grad, keys_grad, value_grad)):
            grad_ref[:, part * width + start : part * width + start + HEAD_DIM] = grad.astype(low)
    spare = joined_width - 3 * width
    if spare:
        grad_ref[:, 3 * width :] = jnp.zeros((rows, spare), low)
    joined_grad = grad_ref[...]
    bias_ref[0] = column_sum(joined_grad.astype(wide))
    out_ref[...] = product_right(joined_grad, weight_ref[:, :joined_width]).astype(low)


def middle_kernel(x_ref, mine_ref, theirs_ref, bias_ref, mod_ref, middle_ref, hidden_ref):
    branch = mine_ref[...].astype(wide) + theirs_ref[...].astype(wide) + bias_ref[...]
    middle = x_ref[...].astype(wide) + mod_ref[0, 2:3] * branch
    middle_ref[...] = middle
    normed, _ = layer_norm(middle)
    hidden_ref[...] = (normed * (1.0 + mod_ref[0, 4:5]) + mod_ref[0, 3:4]).astype(low)


def split_halves(place_ref, partial_ref, keep_ref, send_ref):
    tensor = place_ref[0]
    half = keep_ref.shape[1]
    keep_ref[0] = partial_ref[pl.ds(pl.multiple_of(tensor * half, 8), half), :].astype(low)
    send_ref[0] = partial_ref[pl.ds(pl.multiple_of((1 - tensor) * half, 8), half), :].astype(low)


def gelu_parts(values):
    root = 0.7978845608028654
    square = values * values
    bend = jnp.tanh(root * (values + 0.044715 * values * square))
    return (bend, root * (1.0 + 3.0 * 0.044715 * square))


def units_kernel(
    place_ref,
    hidden_ref,
    up_ref,
    down_ref,
    bias_ref,
    inner_ref,
    active_ref,
    keep_ref,
    send_ref,
    partial_ref,
):
    inner = product(hidden_ref[...], up_ref[...]) + bias_ref[...]
    inner_ref[...] = inner
    bend, _ = gelu_parts(inner)
    active = (0.5 * inner * (1.0 + bend)).astype(low)
    active_ref[...] = active
    partial_ref[...] = product_right(active, down_ref[...])
    split_halves(place_ref, partial_ref, keep_ref, send_ref)


def units_back_kernel(
    place_ref,
    upstream_ref,
    up_ref,
    down_ref,
    inner_ref,
    grad_ref,
    keep_ref,
    send_ref,
    bias_ref,
    partial_ref,
):
    inner = inner_ref[...]
    bend, slope = gelu_parts(inner)
    derivative = 0.5 * (1.0 + bend) + 0.5 * inner * (1.0 - bend * bend) * slope
    grad = (product(upstream_ref[...], down_ref[...]) * derivative).astype(low)
    grad_ref[...] = grad

    @pl.when(pl.program_id(0) == 0)
    def _():
        bias_ref[...] = jnp.zeros_like(bias_ref)

    bias_ref[...] += column_sum(grad.astype(wide))
    partial_ref[...] = product_right(grad, up_ref[...])
    split_halves(place_ref, partial_ref, keep_ref, send_ref)


def result_kernel(middle_ref, branch_ref, bias_ref, mod_ref, out_ref):
    branch = branch_ref[...].astype(wide) + bias_ref[...]
    out_ref[...] = (middle_ref[...] + mod_ref[0, 5:6] * branch).astype(low)


def turn_kernel(upstream_ref, branch_ref, bias_ref, mod_ref, grad_ref, sums_ref):
    upstream = upstream_ref[...].astype(wide)
    branch = branch_ref[...].astype(wide) + bias_ref[...]
    grad = (upstream * mod_ref[0, 5:6]).astype(low)
    grad_ref[...] = grad
    sums_ref[0, 0:1] = column_sum(upstream * branch)
    sums_ref[0, 1:2] = column_sum(grad.astype(wide))


def middle_back_kernel(
    upstream_ref,
    hidden_ref,
    middle_ref,
    mine_ref,
    theirs_ref,
    bias_ref,
    mod_ref,
    out_ref,
    grad_ref,
    sums_ref,
):
    normed, inverse = layer_norm(middle_ref[...])
    hidden_grad = hidden_ref[...].astype(wide)
    middle_grad = upstream_ref[...].astype(wide) + layer_norm_back(
        normed, inverse, hidden_grad * (1.0 + mod_ref[0, 4:5])
    )
    out_ref[...] = middle_grad
    grad = (middle_grad * mod_ref[0, 2:3]).astype(low)
    grad_ref[...] = grad
    branch = mine_ref[...].astype(wide) + theirs_ref[...].astype(wide) + bias_ref[...]
    sums_ref[0, 0:1] = column_sum(hidden_grad)
    sums_ref[0, 1:2] = column_sum(hidden_grad * normed)
    sums_ref[0, 2:3] = column_sum(middle_grad * branch)
    sums_ref[0, 3:4] = column_sum(grad.astype(wide))


def input_back_kernel(middle_ref, mine_ref, theirs_ref, x_ref, mod_ref, out_ref, sums_ref):
    normed, inverse = layer_norm(x_ref[...].astype(wide))
    hidden_grad = mine_ref[...].astype(wide) + theirs_ref[...].astype(wide)
    out_ref[...] = (
        middle_ref[...] + layer_norm_back(normed, inverse, hidden_grad * (1.0 + mod_ref[0, 1:2]))
    ).astype(out_ref.dtype)
    sums_ref[0, 0:1] = column_sum(hidden_grad)
    sums_ref[0, 1:2] = column_sum(hidden_grad * normed)


def array(dtype, *shape):
    return jax.ShapeDtypeStruct(shape, dtype)


def attention_forward(x, mods, weight, bias, place_count):
    rows, width = x.shape
    groups = mods.shape[0]
    block = rows // groups
    part, joined = width // 2, bias.shape[1]
    return pl.pallas_call(
        functools.partial(attention_kernel, place_count),
        grid=(groups,),
        in_specs=[
            by_rows(block, width),
            by_rows(1, 6, width),
            fixed(*weight.shape),
            fixed(*bias.shape),
        ],
        out_specs=[by_rows(block, n) for n in (width, joined, part, width)],
        out_shape=[array(low, rows, n) for n in (width, joined, part, width)],
        name="attention",
        cost_estimate=cost(
            2 * rows * width * (joined + part) + 4 * rows * block * part,
            2 * weight.size + 2 * rows * (3 * width + joined + part),
            rows * block * part // HEAD_DIM,
        ),
    )(x, mods, weight, bias)


def attention_backward(upstream, weight, joined, groups, place_count):
    rows, width = upstream.shape
    block = rows // groups
    columns = joined.shape[1]
    return pl.pallas_call(
        functools.partial(attention_back_kernel, place_count),
        grid=(groups,),
        in_specs=[by_rows(block, width), fixed(*weight.shape), by_rows(block, columns)],
        out_specs=[by_rows(block, columns), by_rows(block, width), by_rows(1, 1, columns)],
        out_shape=[
            array(low, rows, columns),
            array(low, rows, width),
            array(wide, groups, 1, columns),
        ],
        name="attention_back",
        cost_estimate=cost(
            2 * rows * width * weight.shape[1] + 5 * rows * block * width,
            2 * weight.size + 2 * rows * (2 * width + 2 * columns),
            rows * block * width // (2 * HEAD_DIM),
        ),
    )(upstream, weight, joined)


def row_kernel(body, groups, row_inputs, fixed_inputs, mods, outs, sums, name):
    rows, width = row_inputs[0].shape
    block = rows // groups
    sum_shape = [array(wide, groups, 8, width)] * sums
    moved = sum(item.size * item.dtype.itemsize for item in row_inputs)
    return pl.pallas_call(
        body,
        grid=(groups,),
        in_specs=[by_rows(block, width) for _ in row_inputs]
        + [fixed(*item.shape) for item in fixed_inputs]
        + [by_rows(1, 6, width)],
        out_specs=[by_rows(block, width) for _ in outs] + [by_rows(1, 8, width)] * sums,
        out_shape=[array(dtype, rows, width) for dtype in outs] + sum_shape,
        name=name,
        cost_estimate=cost(20 * rows * width, moved + 4 * rows * width * len(outs)),
    )(*row_inputs, *fixed_inputs, mods)


def units_call(body, rows_in, up, down, extra, extra_spec, outs, out_specs, name):
    rows, width = rows_in.shape
    units = up.shape[1]
    half = rows // 2
    halves = array(low, 2, half // 2, width)
    at = pl.BlockSpec((1, half // 2, width), lambda i, *_: (i, 0, 0))
    return pl.pallas_call(
        body,
        grid_spec=pltpu.PrefetchScalarGridSpec(
            num_scalar_prefetch=1,
            grid=(2,),
            in_specs=[
                by_rows(half, width),
                fixed(width, units),
                fixed(width, units),
                extra_spec,
            ],
            out_specs=out_specs[: len(outs) - 1] + [at, at] + out_specs[len(outs) - 1 :]
            if name == "units_back"
            else out_specs + [at, at],
            scratch_shapes=[pltpu.VMEM((half, width), wide)],
        ),
        out_shape=outs[:-1] + [halves, halves] + outs[-1:]
        if name == "units_back"
        else outs + [halves, halves],
        name=name,
        cost_estimate=cost(
            4 * rows * width * units,
            4 * width * units + 4 * rows * width + 6 * rows * units,
            rows * units,
        ),
    )(place_scalars(), rows_in, up, down, extra)


def units_forward(hidden, up, down, bias):
    rows, units = hidden.shape[0], up.shape[1]
    block = by_rows(rows // 2, units)
    return units_call(
        units_kernel,
        hidden,
        up,
        down,
        bias,
        fixed(1, units),
        [array(wide, rows, units), array(low, rows, units)],
        [block, block],
        "units",
    )


def units_backward(upstream, up, down, inner):
    rows, units = inner.shape
    block = by_rows(rows // 2, units)
    return units_call(
        units_back_kernel,
        upstream,
        up,
        down,
        inner,
        block,
        [array(low, rows, units), array(wide, 1, units)],
        [block, fixed(1, units)],
        "units_back",
    )


def block_forward(x, mods, weights, biases, place_count):
    wattn, up, down = weights
    bias_joined, bias_out, bias_fc2, bias_fc1 = biases
    groups = mods.shape[0]
    hidden_attn, joined, attended, mine = attention_forward(
        x, mods, wattn, bias_joined, place_count
    )
    theirs = swap_tensor(mine)
    middle, hidden_mlp = row_kernel(
        middle_kernel, groups, (x, mine, theirs), (bias_out,), mods, (wide, low), 0, "middle"
    )
    flat_mlp = pair_rows(hidden_mlp)
    inner, active, keep, send = units_forward(flat_mlp, up, down, bias_fc1)
    branch_mlp = pair_sum(keep, send)
    (result,) = row_kernel(
        result_kernel, groups, (middle, branch_mlp), (bias_fc2,), mods, (low,), 0, "result"
    )
    saved = (
        x,
        hidden_attn,
        joined,
        attended,
        mine,
        theirs,
        middle,
        flat_mlp,
        inner,
        active,
        branch_mlp,
    )
    return (result, saved)


def block_backward(upstream, saved, mods, weights, biases, place_count, grad_dtype):
    x, hidden_attn, joined, attended, mine, theirs, middle, flat_mlp, inner, active, branch = saved
    wattn, up, down = weights
    _, bias_out, bias_fc2, _ = biases
    groups, width = mods.shape[0], x.shape[1]
    part_width = width // 2
    mlp_grad, turn_sums = row_kernel(
        turn_kernel, groups, (upstream, branch), (bias_fc2,), mods, (low,), 1, "turn"
    )
    flat_grad = pair_rows(mlp_grad)
    inner_grad, keep, send, fc1_bias = units_backward(flat_grad, up, down, inner)
    units_reduced = scatter_product([(flat_mlp, inner_grad), (flat_grad, active)], True)
    hidden_grad = pair_sum(keep, send)
    middle_grad, attn_grad, middle_sums = row_kernel(
        middle_back_kernel,
        groups,
        (upstream, hidden_grad, middle, mine, theirs),
        (bias_out,),
        mods,
        (wide, low),
        1,
        "middle_back",
    )
    joined_grad, mine_grad, joined_bias = attention_backward(
        attn_grad, wattn, joined, groups, place_count
    )
    attn_reduced = scatter_product([(hidden_attn, joined_grad), (attn_grad, attended)], False)
    theirs_grad = swap_tensor(mine_grad)
    input_grad, input_sums = row_kernel(
        input_back_kernel,
        groups,
        (middle_grad, mine_grad, theirs_grad, x),
        (),
        mods,
        (grad_dtype,),
        1,
        "input_back",
    )
    mod_grad = 0.5 * jnp.concatenate(
        [input_sums[:, :2], middle_sums[:, 2:3], middle_sums[:, :2], turn_sums[:, :1]], axis=1
    )
    joined_bias = jnp.sum(joined_bias, axis=(0, 1))
    at = lax.axis_index("tensor") * part_width
    proj_grad = jnp.stack(
        [
            widen(joined_bias[:part_width], at, width),
            widen(joined_bias[2 * part_width : 3 * part_width], at, width),
            0.5 * jnp.sum(middle_sums[:, 3], axis=0),
            0.5 * jnp.sum(turn_sums[:, 1], axis=0),
        ]
    )
    units = fc1_bias.shape[1]
    hidden_bias = widen(fc1_bias[0], unit_start(units), units * 4)
    return (input_grad, mod_grad, (attn_reduced, units_reduced), proj_grad, hidden_bias)


def widen(local_part, offset, total):
    return lax.dynamic_update_slice_in_dim(jnp.zeros((total,), wide), local_part, offset, 0)


def tensor_part(values):
    part = values.shape[-1] // 2
    return lax.dynamic_slice_in_dim(
        values, lax.axis_index("tensor") * part, part, values.ndim - 1
    )


def per_device(tokens, cond, out_grad, w_qkv, w_out, w_fc1, w_fc2, w_ada, b_ada, b_proj, b_fc1):
    dp_count = lax.axis_size("dp")
    all_devices = lax.axis_size(everyone)
    flat_index = lax.axis_index(everyone)
    tensor = lax.axis_index("tensor")
    width = tokens.shape[3]
    clip_count = cond.shape[0]
    own_rows, head_width = w_qkv.shape[1], w_qkv.shape[3]
    units = w_fc1.shape[2] // 2
    own_width = width // all_devices
    own_start = flat_index * own_width
    joined_width = 3 * head_width

    def pad_columns(values):
        return jnp.pad(values, ((0, 0), (0, padded(values.shape[1]) - values.shape[1])))

    def units_part(layer, side):
        first = side * units
        return jnp.concatenate(
            [
                lax.dynamic_slice_in_dim(w_fc1[layer], first, units, 1),
                lax.dynamic_slice_in_dim(w_fc2[layer], first, units, 0).T,
            ],
            axis=1,
        )

    shards = []
    for layer in range(2):
        shards.append(
            jnp.concatenate(
                [
                    pad_columns(w_qkv[layer].reshape(own_rows, joined_width)),
                    pad_columns(w_out[layer].T),
                ],
                axis=1,
            )
        )
        shards.append((units_part(layer, my_bit(PAIR)), units_part(layer, 1 - my_bit(PAIR))))
    full = gather_all(shards, dp_count)
    gathered = [
        (full[2 * layer], full[2 * layer + 1][:, :units], full[2 * layer + 1][:, units:])
        for layer in range(2)
    ]

    cond_float = cond.astype(wide)
    gated_low = jax.nn.silu(cond_float).astype(low)
    gated_own = lax.dynamic_slice_in_dim(gated_low, own_start, own_width, 1).astype(wide)
    w_ada_wide = w_ada.astype(wide)
    partial_mod = jnp.stack(
        [
            jnp.sum(gated_own[clip][None, :, None, None] * w_ada_wide, axis=1)
            for clip in range(clip_count)
        ],
        axis=1,
    )
    own_mod = jnp.sum(deal(sum_to_owner(partial_mod, all_devices)), axis=0).reshape(
        2, clip_count, 6, own_width
    )
    own_mod = own_mod + b_ada.astype(wide)[:, None]
    pieces = (own_mod, b_proj.astype(wide), b_fc1.astype(wide))
    packed = jnp.concatenate([piece.reshape(-1) for piece in pieces])
    dealt = deal(jnp.broadcast_to(packed[None], (all_devices, packed.shape[0])))
    first_end, second_end = pieces[0].size, pieces[0].size + pieces[1].size
    modulation = from_owners(dealt[:, :first_end], (2, clip_count, 6))
    proj_full = from_owners(dealt[:, first_end:second_end], (2, 4))
    hidden_full = from_owners(dealt[:, second_end:], (2,))

    frames_dev, place_half = tokens.shape[0], tokens.shape[2]
    frame_ids = lax.axis_index("dp") * frames_dev + jnp.arange(frames_dev, dtype=jnp.int32)
    onehot = (
        frame_ids[:, None] // FRAMES == jnp.arange(clip_count, dtype=jnp.int32)[None, :]
    ).astype(wide)
    first_mod = jnp.sum(onehot[:, :, None, None] * modulation[0][None], axis=1)
    second_mod = modulation[1]

    def layer_biases(layer):
        bias_query = tensor_part(proj_full[layer, 0])
        bias_value = tensor_part(proj_full[layer, 1])
        joined = jnp.concatenate([bias_query, jnp.zeros_like(bias_query), bias_value])
        return (
            jnp.pad(joined, (0, padded(joined_width) - joined_width))[None],
            proj_full[layer, 2:3],
            proj_full[layer, 3:4],
            lax.dynamic_slice_in_dim(hidden_full[layer], unit_start(units), units)[None],
        )

    def flat(values):
        return both_halves(values).reshape(-1, width)

    def own_places(values, frames):
        split = values.reshape(frames, 2, -1, width)
        return lax.dynamic_slice_in_dim(split, tensor, 1, 1)

    all_frames, own_place_count = frames_dev * dp_count, 2 * (place_half // dp_count)
    first_x = flat(tokens)
    first_biases, second_biases = layer_biases(0), layer_biases(1)
    first_out, first_saved = block_forward(first_x, first_mod, gathered[0], first_biases, None)
    arrived = lax.all_to_all(
        own_places(first_out, frames_dev), "dp", split_axis=2, concat_axis=0, tiled=True
    )
    second_out, second_saved = block_forward(
        flat(arrived), second_mod, gathered[1], second_biases, own_place_count
    )
    output = own_places(second_out, all_frames)

    second_grad, second_dmod, second_reduced, second_proj, second_hidden = block_backward(
        flat(out_grad), second_saved, second_mod, gathered[1], second_biases, own_place_count, low
    )
    arrived_back = lax.all_to_all(
        own_places(second_grad, all_frames), "dp", split_axis=0, concat_axis=2, tiled=True
    )
    first_grad, first_dmod, first_reduced, first_proj, first_hidden = block_backward(
        flat(arrived_back), first_saved, first_mod, gathered[0], first_biases, None, wide
    )
    tokens_grad = own_places(first_grad, frames_dev)

    dmod_clips = jnp.stack(
        [jnp.sum(onehot[:, :, None, None] * first_dmod[:, None], axis=0), second_dmod]
    )
    small = (
        dmod_clips,
        jnp.stack([first_proj, second_proj]),
        jnp.stack([first_hidden, second_hidden]),
    )
    owned = jnp.sum(
        deal(jnp.concatenate([sum_to_owner(piece, all_devices) for piece in small], axis=1)), axis=0
    )
    own_dmod = owned[:first_end]
    b_proj_grad = owned[first_end:second_end].reshape(2, 4, own_width)
    b_fc1_grad = owned[second_end:].reshape(2, -1)
    summed_mod = from_owners(
        deal(jnp.broadcast_to(own_dmod[None], (all_devices, own_dmod.shape[0]))), (2, clip_count, 6)
    )
    w_ada_grad = sum(
        gated_own[clip][None, :, None, None] * summed_mod[:, clip][:, None]
        for clip in range(clip_count)
    )
    b_ada_grad = jnp.sum(own_dmod.reshape(2, clip_count, 6, own_width), axis=1)
    silu_grad = jnp.stack(
        [
            jnp.sum(summed_mod[:, clip][:, None] * w_ada_wide, axis=(0, 2, 3))
            for clip in range(clip_count)
        ]
    )
    cond_own = lax.dynamic_slice_in_dim(cond_float, own_start, own_width, 1)
    cond_grad = jax.vjp(jax.nn.silu, cond_own)[1](silu_grad)[0]

    reduced = (first_reduced, second_reduced)
    out_start = padded(joined_width)
    w_qkv_grad = jnp.stack(
        [part[0][:, :joined_width].reshape(own_rows, 3, head_width) for part in reduced]
    )
    w_out_grad = jnp.stack(
        [part[0][:, out_start : out_start + head_width].T for part in reduced]
    )
    w_fc1_grad = jnp.stack(
        [jnp.concatenate([part[1][0, :, :units], part[1][1, :, :units]], axis=1) for part in reduced]
    )
    w_fc2_grad = jnp.stack(
        [part[1][:, :, units:].transpose(0, 2, 1).reshape(2 * units, own_rows) for part in reduced]
    )
    return (
        output,
        tokens_grad,
        cond_grad,
        w_qkv_grad,
        w_out_grad,
        w_fc1_grad,
        w_fc2_grad,
        w_ada_grad,
        b_ada_grad,
        b_proj_grad,
        b_fc1_grad,
    )


def solution(mesh):
    return jax.shard_map(
        per_device,
        mesh=mesh,
        in_specs=(
            P("dp", "tensor", None, None),
            P(),
            P(None, "tensor", "dp", None),
            P(None, "dp", None, "tensor"),
            P(None, "tensor", "dp"),
            P(None, "dp", "tensor"),
            P(None, "tensor", "dp"),
            P(None, ("dp", "tensor"), None, None),
            P(None, None, ("dp", "tensor")),
            P(None, None, ("dp", "tensor")),
            P(None, ("dp", "tensor")),
        ),
        out_specs=(
            P(None, "tensor", "dp", None),
            P("dp", "tensor", None, None),
            P(None, ("dp", "tensor")),
            P(None, "dp", None, "tensor"),
            P(None, "tensor", "dp"),
            P(None, "dp", "tensor"),
            P(None, "tensor", "dp"),
            P(None, ("dp", "tensor"), None, None),
            P(None, None, ("dp", "tensor")),
            P(None, None, ("dp", "tensor")),
            P(None, ("dp", "tensor")),
        ),
        check_vma=False,
    )
```

```python
import functools

import jax
import jax.numpy as jnp
from jax import lax
from jax.experimental import pallas as pl
from jax.experimental.pallas import tpu as pltpu
from jax.sharding import PartitionSpec as P

HEAD_DIM = 72
FRAMES = 16


epsilon = 1e-06
highest = lax.Precision.HIGHEST
low = jnp.bfloat16
wide = jnp.float32
everyone = ("dp", "tensor")


def layer_norm(values):
    centred = values - jnp.mean(values, axis=-1, keepdims=True)
    inverse = lax.rsqrt(jnp.mean(centred * centred, axis=-1, keepdims=True) + epsilon)
    return (centred * inverse, inverse)


def layer_norm_back(normed, inverse, upstream):
    first_moment = jnp.mean(upstream, axis=-1, keepdims=True)
    second_moment = jnp.mean(upstream * normed, axis=-1, keepdims=True)
    return inverse * (upstream - first_moment - normed * second_moment)


def product(left_side, right_side):
    return jnp.dot(left_side, right_side, preferred_element_type=wide)


def product_left(left_side, right_side):
    return lax.dot_general(
        left_side, right_side, (((0,), (0,)), ((), ())), preferred_element_type=wide
    )


def product_right(left_side, right_side):
    return lax.dot_general(
        left_side, right_side, (((1,), (1,)), ((), ())), preferred_element_type=wide
    )


PAIR = 2


def swap_by(values, offset):
    count = lax.axis_size("dp")
    return lax.ppermute(values, "dp", [(i, i ^ offset) for i in range(count)])


def my_bit(bit):
    return (lax.axis_index("dp") >> bit) & 1


def after(values, *others):
    return lax.optimization_barrier((values,) + others)[0]


def pick(first, mine, theirs, axis):
    return jnp.stack(
        [jnp.where(first, mine, theirs), jnp.where(first, theirs, mine)], axis=axis
    )


def place_scalars():
    return jnp.stack(
        [lax.axis_index("tensor"), lax.axis_index("dp") & 3, lax.axis_index("dp") >> 2]
    ).astype(jnp.int32)


def gather_pair(shard):
    paired = isinstance(shard, tuple)
    own, sent = shard if paired else (shard, shard)
    return jnp.stack([own, swap_by(sent, 1 << PAIR)])


def gather_planes(held):
    while held.shape[0] * 4 < lax.axis_size("dp"):
        held = jnp.concatenate([held, swap_by(held, held.shape[0] * 4)])
    return held


def gather_straight(shard):
    paired = isinstance(shard, tuple)
    parts = [shard[0] if paired else shard]
    for relative in range(1, lax.axis_size("dp") // 4):
        sent = shard[relative & 1] if paired else shard
        parts.append(swap_by(sent, relative << 2))
    return jnp.stack(parts)


def arrange_kernel(place_ref, own_ref, across_ref, along_ref, low_ref, high_ref, out_ref):
    me = place_ref[1]
    out_ref[me] = own_ref[0]
    out_ref[me ^ 1] = across_ref[0]
    out_ref[me ^ 2] = along_ref[0]
    in_low = pl.program_id(0) < pl.num_programs(0) // 2

    @pl.when(in_low)
    def _():
        out_ref[me ^ 3] = low_ref[0]

    @pl.when(jnp.logical_not(in_low))
    def _():
        out_ref[me ^ 3] = high_ref[0]


def arrange(own, across, along, low_part, high_part):
    groups, rows, columns = own.shape
    half = groups // 2
    block = (1, rows, columns)
    whole = pl.BlockSpec(block, lambda i, place: (i, 0, 0))
    out = pl.pallas_call(
        arrange_kernel,
        out_shape=jax.ShapeDtypeStruct((groups * 4, rows, columns), own.dtype),
        grid_spec=pltpu.PrefetchScalarGridSpec(
            num_scalar_prefetch=1,
            grid=(groups,),
            in_specs=[
                whole,
                whole,
                whole,
                pl.BlockSpec(block, lambda i, place: (jnp.minimum(i, half - 1), 0, 0)),
                pl.BlockSpec(block, lambda i, place: (jnp.maximum(i - half, 0), 0, 0)),
            ],
            out_specs=pl.BlockSpec((4, rows, columns), lambda i, place: (i ^ place[2], 0, 0)),
        ),
        name="arrange",
        cost_estimate=cost(0, 16 * groups * rows * columns),
    )(place_scalars(), own, across, along, low_part, high_part)
    return out.reshape(groups * 4 * rows, columns)


def gather_near(own):
    return (own, swap_by(own, 1), swap_by(own, 2))


def gather_halves(near):
    half = near[0].shape[0] // 2
    return (near[1][:half], near[2][half:])


def gather_far(halves):
    return (swap_by(halves[0], 2), swap_by(halves[1], 1))


def together(*values):
    return lax.optimization_barrier(values)


def weight_grad_kernel(count, starts, place_ref, *refs):
    pairs = len(starts)
    operands, outs, total = refs[: 2 * pairs], refs[2 * pairs : -1], refs[-1]
    own, to_across, to_along, rest_across, rest_along = outs
    me, plane = place_ref[1], place_ref[2]
    rows, groups = total.shape[0] // count, count // 4
    half = groups // 2
    for index, start in enumerate(starts):
        left, right = operands[2 * index], operands[2 * index + 1]
        total[:, start : start + right.shape[1]] = product_left(left[...], right[...])
        spare = -right.shape[1] % 128
        if spare:
            end = start + right.shape[1]
            total[:, end : end + spare] = jnp.zeros((total.shape[0], spare), wide)

    def copy(out, at, mate, first, length):
        place = me ^ mate
        if rows % 8 == 0:

            @pl.loop(0, length)
            def _(step):
                chip = (plane ^ (first + step)) * 4 + place
                out[at + step] = total[pl.ds(pl.multiple_of(chip * rows, 8), rows), :].astype(low)

        else:

            for chip in range(count):

                @pl.when((chip & 3) == place)
                def _(chip=chip):
                    step = (plane ^ (chip >> 2)) - first

                    @pl.when((step >= 0) & (step < length))
                    def _():
                        out[at + step] = total[chip * rows : (chip + 1) * rows, :].astype(low)

    copy(to_along, 0, 3, 0, half)
    copy(to_along, half, 2, 0, half)
    copy(to_across, 0, 3, half, half)
    copy(to_across, half, 1, half, half)
    copy(rest_across, 0, 1, 0, half)
    copy(rest_along, 0, 2, half, half)
    copy(own, 0, 0, 0, groups)


def weight_grad(pairs):
    count = lax.axis_size("dp")
    groups = count // 4
    half = groups // 2
    width = pairs[0][0].shape[1]
    rows = width // count
    starts, columns = [], 0
    for _, right in pairs:
        starts.append(columns)
        columns += padded(right.shape[1])
    tokens = pairs[0][0].shape[0]
    own, to_across, to_along, rest_across, rest_along = pl.pallas_call(
        functools.partial(weight_grad_kernel, count, tuple(starts)),
        out_shape=[
            jax.ShapeDtypeStruct((blocks, rows, columns), low)
            for blocks in (groups, groups, groups, half, half)
        ],
        in_specs=[pl.BlockSpec(memory_space=pltpu.SMEM)]
        + [pl.BlockSpec(memory_space=pltpu.VMEM)] * (2 * len(pairs)),
        scratch_shapes=[pltpu.VMEM((width, columns), wide)],
        name="weight_grad",
        cost_estimate=cost(
            2 * tokens * width * columns, 2 * width * columns + 4 * tokens * (width + columns)
        ),
    )(place_scalars(), *[operand for pair in pairs for operand in pair])
    return (own, rest_across, rest_along, to_across, to_along)


def scatter_start(parts):
    own, rest_across, rest_along, to_across, to_along = parts
    return (own, rest_across, rest_along, swap_by(to_across, 1), swap_by(to_along, 2))


def scatter_near(state):
    own, rest_across, rest_along, got_across, got_along = state
    half = rest_across.shape[0]
    rest_across = (rest_across.astype(wide) + got_along[:half].astype(wide)).astype(low)
    rest_along = (rest_along.astype(wide) + got_across[:half].astype(wide)).astype(low)
    return (own, got_across, got_along, swap_by(rest_across, 1), swap_by(rest_along, 2))


def scatter_plane_blocks(state):
    own, got_across, got_along, last_across, last_along = state
    half = own.shape[0] // 2

    def total(relative):
        block = own[relative].astype(wide)
        if relative < half:
            return block + got_along[half + relative].astype(wide) + last_across[relative].astype(wide)
        return block + got_across[relative].astype(wide) + last_along[relative - half].astype(wide)

    return [total(relative) for relative in range(own.shape[0])]


def scatter_planes(state):
    blocks = scatter_plane_blocks(state)
    got = [
        swap_by(block.astype(low), relative << 2) for relative, block in enumerate(blocks) if relative
    ]
    return (blocks[0], got)


def scatter_finish(state):
    own, got = state
    return own + sum(part.astype(wide) for part in got)


def scatter_halve(blocks):
    half = len(blocks) // 2
    sent = jnp.stack([block.astype(low) for block in blocks[half:]])
    return (blocks[:half], swap_by(sent, half * 4))


def scatter_join(state, paired=False):
    kept, got = state
    if paired:
        return pick(my_bit(PAIR) == 0, kept[0], got[0].astype(wide), 0)
    return [block + got[index].astype(wide) for index, block in enumerate(kept)]


def scatter_last(state):
    blocks = scatter_join(state)
    while len(blocks) > 2:
        blocks = scatter_join(scatter_halve(blocks))
    return scatter_halve(blocks)


def swap_tensor(values):
    return lax.ppermute(values, "tensor", [(0, 1), (1, 0)])


def both_halves(values):
    return lax.all_gather(values, "tensor", axis=1, tiled=True)


def own_half(values):
    return lax.dynamic_slice_in_dim(
        values, lax.axis_index("tensor") * (values.shape[1] // 2), values.shape[1] // 2, 1
    )


def pair_rows(values):
    half = values.shape[0] // 2
    sent = lax.dynamic_slice_in_dim(values, lax.axis_index("tensor") * half, half, 0)
    got = swap_by(sent, 1 << PAIR)
    return jnp.concatenate([values, lax.all_gather(got, "tensor", axis=0, tiled=True)])


def chip_sum(keep, send):
    return keep.astype(wide) + swap_tensor(send).astype(wide)


def pair_sum(chip):
    got = swap_by(chip[1].astype(low), 1 << PAIR)
    total = (chip[0] + got.astype(wide)).astype(low)
    return lax.all_gather(total, "tensor", axis=0, tiled=True)


def unit_start(units):
    return (lax.axis_index("tensor") * 2 + my_bit(PAIR)) * units


def deal(values):
    return lax.all_to_all(values, everyone, split_axis=0, concat_axis=0, tiled=True)


def sum_to_owner(values, owners):
    lead = values.shape[:-1]
    dealt = jnp.moveaxis(values.reshape(lead + (owners, -1)), -2, 0)
    return dealt.reshape(owners, -1)


def from_owners(values, lead):
    owners = values.shape[0]
    return jnp.moveaxis(values.reshape((owners,) + lead + (-1,)), 0, -2).reshape(lead + (-1,))


def padded(width):
    return width + -width % 128


def fixed(*shape):
    return pl.BlockSpec(shape, lambda i, *_: (0,) * len(shape))


def by_rows(rows, *rest):
    return pl.BlockSpec((rows,) + rest, lambda i, *_: (i,) + (0,) * len(rest))


COST_SHARE = 16


def cost(flops, bytes_accessed, transcendentals=0):
    return pl.CostEstimate(
        flops=flops // COST_SHARE,
        bytes_accessed=bytes_accessed // COST_SHARE,
        transcendentals=transcendentals // COST_SHARE,
    )


def column_sum(values):
    return jnp.sum(values, axis=0, keepdims=True)


def same_place(rows, place_count):
    if rows == place_count:
        return None
    first = lax.broadcasted_iota(jnp.int32, (rows, rows), 0)
    second = lax.broadcasted_iota(jnp.int32, (rows, rows), 1)
    return lax.rem(first, place_count) == lax.rem(second, place_count)


def head_probs(query, keys, mask):
    scores = product_right(query, keys) * (HEAD_DIM ** (-0.5))
    if mask is not None:
        scores = jnp.where(mask, scores, -1e30)
    exponent = jnp.exp(scores - jnp.max(scores, axis=-1, keepdims=True))
    return exponent * (1.0 / jnp.sum(exponent, axis=-1, keepdims=True))


def attention_kernel(
    place_count, x_ref, mod_ref, weight_ref, bias_ref, hidden_ref, joined_ref, attended_ref, out_ref
):
    rows, width = attended_ref.shape
    joined_width = joined_ref.shape[1]
    normed, _ = layer_norm(x_ref[...].astype(wide))
    hidden = (normed * (1.0 + mod_ref[0, 1:2]) + mod_ref[0, 0:1]).astype(low)
    hidden_ref[...] = hidden
    joined_ref[...] = (product(hidden, weight_ref[:, :joined_width]) + bias_ref[...]).astype(low)
    mask = None if place_count is None else same_place(rows, place_count)
    for start in range(0, width, HEAD_DIM):
        query, keys, value = (
            joined_ref[:, part * width + start : part * width + start + HEAD_DIM]
            for part in range(3)
        )
        probs = head_probs(query, keys, mask).astype(low)
        attended_ref[:, start : start + HEAD_DIM] = product(probs, value).astype(low)
    out_ref[...] = product_right(
        attended_ref[...], weight_ref[:, joined_width : joined_width + width]
    ).astype(low)


def attention_back_kernel(
    place_count, upstream_ref, weight_ref, joined_ref, grad_ref, out_ref, bias_ref
):
    rows, joined_width = joined_ref.shape
    width = upstream_ref.shape[1] // 2
    score_scale = HEAD_DIM ** (-0.5)
    attended_grad = product(
        upstream_ref[...], weight_ref[:, joined_width : joined_width + width]
    ).astype(low)
    mask = None if place_count is None else same_place(rows, place_count)
    for start in range(0, width, HEAD_DIM):
        query, keys, value = (
            joined_ref[:, part * width + start : part * width + start + HEAD_DIM]
            for part in range(3)
        )
        upstream = attended_grad[:, start : start + HEAD_DIM]
        probs = head_probs(query, keys, mask)
        value_grad = product_left(probs.astype(low), upstream)
        prob_grad = product_right(upstream, value)
        centre = jnp.sum(probs * prob_grad, axis=-1, keepdims=True)
        score_grad = (probs * (prob_grad - centre)).astype(low)
        query_grad = product(score_grad, keys) * score_scale
        keys_grad = product_left(score_grad, query) * score_scale
        for part, grad in enumerate((query_grad, keys_grad, value_grad)):
            grad_ref[:, part * width + start : part * width + start + HEAD_DIM] = grad.astype(low)
    spare = joined_width - 3 * width
    if spare:
        grad_ref[:, 3 * width :] = jnp.zeros((rows, spare), low)
    joined_grad = grad_ref[...]
    bias_ref[0] = column_sum(joined_grad.astype(wide))
    out_ref[...] = product_right(joined_grad, weight_ref[:, :joined_width]).astype(low)


def middle_kernel(x_ref, mine_ref, theirs_ref, bias_ref, mod_ref, middle_ref, hidden_ref):
    branch = mine_ref[...].astype(wide) + theirs_ref[...].astype(wide) + bias_ref[...]
    middle = x_ref[...].astype(wide) + mod_ref[0, 2:3] * branch
    middle_ref[...] = middle
    normed, _ = layer_norm(middle)
    hidden_ref[...] = (normed * (1.0 + mod_ref[0, 4:5]) + mod_ref[0, 3:4]).astype(low)


def split_halves(place_ref, partial_ref, keep_ref, send_ref):
    tensor = place_ref[0]
    half = keep_ref.shape[1]
    keep_ref[0] = partial_ref[pl.ds(pl.multiple_of(tensor * half, 8), half), :].astype(low)
    send_ref[0] = partial_ref[pl.ds(pl.multiple_of((1 - tensor) * half, 8), half), :].astype(low)


def gelu_parts(values):
    root = 0.7978845608028654
    square = values * values
    bend = jnp.tanh(root * (values + 0.044715 * values * square))
    share = 0.5 * (1.0 + bend)
    steep = 0.5 * root * (1.0 - bend * bend) * (1.0 + 3.0 * 0.044715 * square)
    return (values * share, share + values * steep)


def units_kernel(
    place_ref,
    hidden_ref,
    up_ref,
    down_ref,
    bias_ref,
    slope_ref,
    active_ref,
    keep_ref,
    send_ref,
    partial_ref,
):
    inner = product(hidden_ref[...], up_ref[...]) + bias_ref[...]
    active, slope = gelu_parts(inner)
    slope_ref[...] = slope.astype(low)
    active = active.astype(low)
    active_ref[...] = active
    partial_ref[...] = product_right(active, down_ref[...])
    split_halves(place_ref, partial_ref, keep_ref, send_ref)


def units_back_kernel(
    place_ref,
    upstream_ref,
    up_ref,
    down_ref,
    slope_ref,
    grad_ref,
    keep_ref,
    send_ref,
    bias_ref,
    partial_ref,
):
    grad = (product(upstream_ref[...], down_ref[...]) * slope_ref[...].astype(wide)).astype(low)
    grad_ref[...] = grad

    @pl.when(pl.program_id(0) == 0)
    def _():
        bias_ref[...] = jnp.zeros_like(bias_ref)

    bias_ref[...] += column_sum(grad.astype(wide))
    partial_ref[...] = product_right(grad, up_ref[...])
    split_halves(place_ref, partial_ref, keep_ref, send_ref)


def result_kernel(middle_ref, branch_ref, bias_ref, mod_ref, out_ref):
    branch = branch_ref[...].astype(wide) + bias_ref[...]
    out_ref[...] = (middle_ref[...] + mod_ref[0, 5:6] * branch).astype(low)


def turn_kernel(upstream_ref, mod_ref, grad_ref, sums_ref):
    grad = (upstream_ref[...].astype(wide) * mod_ref[0, 5:6]).astype(low)
    grad_ref[...] = grad
    sums_ref[0, 0:1] = column_sum(grad.astype(wide))


def gate_kernel(upstream_ref, branch_ref, bias_ref, mod_ref, sums_ref):
    branch = branch_ref[...].astype(wide) + bias_ref[...]
    sums_ref[0, 0:1] = column_sum(upstream_ref[...].astype(wide) * branch)


def middle_back_kernel(
    upstream_ref,
    hidden_ref,
    middle_ref,
    mine_ref,
    theirs_ref,
    bias_ref,
    mod_ref,
    out_ref,
    grad_ref,
    sums_ref,
):
    normed, inverse = layer_norm(middle_ref[...])
    hidden_grad = hidden_ref[...].astype(wide)
    middle_grad = upstream_ref[...].astype(wide) + layer_norm_back(
        normed, inverse, hidden_grad * (1.0 + mod_ref[0, 4:5])
    )
    out_ref[...] = middle_grad
    grad = (middle_grad * mod_ref[0, 2:3]).astype(low)
    grad_ref[...] = grad
    branch = mine_ref[...].astype(wide) + theirs_ref[...].astype(wide) + bias_ref[...]
    sums_ref[0, 0:1] = column_sum(hidden_grad)
    sums_ref[0, 1:2] = column_sum(hidden_grad * normed)
    sums_ref[0, 2:3] = column_sum(middle_grad * branch)
    sums_ref[0, 3:4] = column_sum(grad.astype(wide))


def input_back_kernel(middle_ref, mine_ref, theirs_ref, x_ref, mod_ref, out_ref, sums_ref):
    normed, inverse = layer_norm(x_ref[...].astype(wide))
    hidden_grad = mine_ref[...].astype(wide) + theirs_ref[...].astype(wide)
    out_ref[...] = (
        middle_ref[...] + layer_norm_back(normed, inverse, hidden_grad * (1.0 + mod_ref[0, 1:2]))
    ).astype(out_ref.dtype)
    sums_ref[0, 0:1] = column_sum(hidden_grad)
    sums_ref[0, 1:2] = column_sum(hidden_grad * normed)


def array(dtype, *shape):
    return jax.ShapeDtypeStruct(shape, dtype)


def attention_forward(x, mods, weight, bias, place_count):
    rows, width = x.shape
    groups = mods.shape[0]
    block = rows // groups
    part, joined = width // 2, bias.shape[1]
    return pl.pallas_call(
        functools.partial(attention_kernel, place_count),
        grid=(groups,),
        in_specs=[
            by_rows(block, width),
            by_rows(1, 6, width),
            fixed(*weight.shape),
            fixed(*bias.shape),
        ],
        out_specs=[by_rows(block, n) for n in (width, joined, part, width)],
        out_shape=[array(low, rows, n) for n in (width, joined, part, width)],
        name="attention",
        cost_estimate=cost(
            2 * rows * width * (joined + part) + 4 * rows * block * part,
            2 * weight.size + 2 * rows * (3 * width + joined + part),
            rows * block * part // HEAD_DIM,
        ),
    )(x, mods, weight, bias)


def attention_backward(upstream, weight, joined, groups, place_count):
    rows, width = upstream.shape
    block = rows // groups
    columns = joined.shape[1]
    return pl.pallas_call(
        functools.partial(attention_back_kernel, place_count),
        grid=(groups,),
        in_specs=[by_rows(block, width), fixed(*weight.shape), by_rows(block, columns)],
        out_specs=[by_rows(block, columns), by_rows(block, width), by_rows(1, 1, columns)],
        out_shape=[
            array(low, rows, columns),
            array(low, rows, width),
            array(wide, groups, 1, columns),
        ],
        name="attention_back",
        cost_estimate=cost(
            2 * rows * width * weight.shape[1] + 5 * rows * block * width,
            2 * weight.size + 2 * rows * (2 * width + 2 * columns),
            rows * block * width // (2 * HEAD_DIM),
        ),
    )(upstream, weight, joined)


def row_kernel(body, groups, row_inputs, fixed_inputs, mods, outs, sums, name):
    rows, width = row_inputs[0].shape
    block = rows // groups
    sum_shape = [array(wide, groups, 8, width)] * sums
    moved = sum(item.size * item.dtype.itemsize for item in row_inputs)
    return pl.pallas_call(
        body,
        grid=(groups,),
        in_specs=[by_rows(block, width) for _ in row_inputs]
        + [fixed(*item.shape) for item in fixed_inputs]
        + [by_rows(1, 6, width)],
        out_specs=[by_rows(block, width) for _ in outs] + [by_rows(1, 8, width)] * sums,
        out_shape=[array(dtype, rows, width) for dtype in outs] + sum_shape,
        name=name,
        cost_estimate=cost(20 * rows * width, moved + 4 * rows * width * len(outs)),
    )(*row_inputs, *fixed_inputs, mods)


def units_call(body, rows_in, updown, extra, extra_spec, outs, out_specs, name):
    rows, width = rows_in.shape
    units = updown.shape[1] // 2
    half = rows // 2
    halves = array(low, 2, half // 2, width)
    at = pl.BlockSpec((1, half // 2, width), lambda i, *_: (i, 0, 0))
    return pl.pallas_call(
        body,
        grid_spec=pltpu.PrefetchScalarGridSpec(
            num_scalar_prefetch=1,
            grid=(2,),
            in_specs=[
                by_rows(half, width),
                pl.BlockSpec((width, units), lambda i, *_: (0, 0)),
                pl.BlockSpec((width, units), lambda i, *_: (0, 1)),
                extra_spec,
            ],
            out_specs=out_specs[: len(outs) - 1] + [at, at] + out_specs[len(outs) - 1 :]
            if name == "units_back"
            else out_specs + [at, at],
            scratch_shapes=[pltpu.VMEM((half, width), wide)],
        ),
        out_shape=outs[:-1] + [halves, halves] + outs[-1:]
        if name == "units_back"
        else outs + [halves, halves],
        name=name,
        cost_estimate=cost(
            4 * rows * width * units,
            4 * width * units + 4 * rows * width + 6 * rows * units,
            rows * units,
        ),
    )(place_scalars(), rows_in, updown, updown, extra)


def units_forward(hidden, updown, bias):
    rows, units = hidden.shape[0], updown.shape[1] // 2
    block = by_rows(rows // 2, units)
    return units_call(
        units_kernel,
        hidden,
        updown,
        bias,
        fixed(1, units),
        [array(low, rows, units), array(low, rows, units)],
        [block, block],
        "units",
    )


def units_backward(upstream, updown, slope):
    rows, units = slope.shape
    block = by_rows(rows // 2, units)
    return units_call(
        units_back_kernel,
        upstream,
        updown,
        slope,
        block,
        [array(low, rows, units), array(wide, 1, units)],
        [block, fixed(1, units)],
        "units_back",
    )


def first_half(x, mods, wattn, biases, place_count):
    hidden, joined, attended, mine = attention_forward(x, mods, wattn, biases[0], place_count)
    both = (mine, swap_tensor(mine))
    middle, hidden_mlp = row_kernel(
        middle_kernel, mods.shape[0], (x, *both), (biases[1],), mods, (wide, low), 0, "middle"
    )
    return (hidden, joined, attended, both, middle, hidden_mlp)


def block_result(middle, branch, biases, mods):
    return row_kernel(
        result_kernel, mods.shape[0], (middle, branch), (biases[2],), mods, (low,), 0, "result"
    )[0]


def turn(upstream, mods):
    return row_kernel(turn_kernel, mods.shape[0], (upstream,), (), mods, (low,), 1, "turn")


def gate_sums(upstream, branch, biases, mods):
    return row_kernel(
        gate_kernel, mods.shape[0], (upstream, branch), (biases[2],), mods, (), 1, "gate"
    )[0]


def middle_back(upstream, hidden_grad, middle, both, biases, mods):
    return row_kernel(
        middle_back_kernel,
        mods.shape[0],
        (upstream, hidden_grad, middle, *both),
        (biases[1],),
        mods,
        (wide, low),
        1,
        "middle_back",
    )


def input_back(middle_grad, mine_grad, x, mods, grad_dtype):
    return row_kernel(
        input_back_kernel,
        mods.shape[0],
        (middle_grad, mine_grad, swap_tensor(mine_grad), x),
        (),
        mods,
        (grad_dtype,),
        1,
        "input_back",
    )


def small_grads(input_sums, middle_sums, gate, turn_sums, joined_bias, fc1_bias):
    width = gate.shape[2]
    part_width, units = width // 2, fc1_bias.shape[1]
    mod_grad = 0.5 * jnp.concatenate(
        [input_sums[:, :2], middle_sums[:, 2:3], middle_sums[:, :2], gate[:, :1]], axis=1
    )
    joined_bias = jnp.sum(joined_bias, axis=(0, 1))
    at = lax.axis_index("tensor") * part_width
    proj_grad = jnp.stack(
        [
            widen(joined_bias[:part_width], at, width),
            widen(joined_bias[2 * part_width : 3 * part_width], at, width),
            0.5 * jnp.sum(middle_sums[:, 3], axis=0),
            0.5 * jnp.sum(turn_sums[:, 0], axis=0),
        ]
    )
    return (mod_grad, proj_grad, widen(fc1_bias[0], unit_start(units), units * 4))


def widen(local_part, offset, total):
    return lax.dynamic_update_slice_in_dim(jnp.zeros((total,), wide), local_part, offset, 0)


def tensor_part(values):
    part = values.shape[-1] // 2
    return lax.dynamic_slice_in_dim(
        values, lax.axis_index("tensor") * part, part, values.ndim - 1
    )


def per_device(tokens, cond, out_grad, w_qkv, w_out, w_fc1, w_fc2, w_ada, b_ada, b_proj, b_fc1):
    dp_count = lax.axis_size("dp")
    all_devices = lax.axis_size(everyone)
    flat_index = lax.axis_index(everyone)
    tensor = lax.axis_index("tensor")
    width = tokens.shape[3]
    clip_count = cond.shape[0]
    own_rows, head_width = w_qkv.shape[1], w_qkv.shape[3]
    units = w_fc1.shape[2] // 2
    own_width = width // all_devices
    own_start = flat_index * own_width
    joined_width = 3 * head_width

    def pad_columns(values):
        return jnp.pad(values, ((0, 0), (0, padded(values.shape[1]) - values.shape[1])))

    def units_part(layer, side):
        first = side * units
        return jnp.concatenate(
            [
                lax.dynamic_slice_in_dim(w_fc1[layer], first, units, 1),
                lax.dynamic_slice_in_dim(w_fc2[layer], first, units, 0).T,
            ],
            axis=1,
        )

    shards = []
    for layer in range(2):
        shards.append(
            jnp.concatenate(
                [
                    pad_columns(w_qkv[layer].reshape(own_rows, joined_width)),
                    pad_columns(w_out[layer].T),
                ],
                axis=1,
            )
        )
        shards.append((units_part(layer, my_bit(PAIR)), units_part(layer, 1 - my_bit(PAIR))))
    own_attn_0 = gather_straight(shards[0])
    near_attn_0 = gather_near(own_attn_0)
    own_units_0 = gather_straight(after(shards[1], own_attn_0))
    near_units_0 = gather_near(own_units_0)
    far_attn_0 = gather_far(gather_halves(near_attn_0))
    own_attn_1 = gather_planes(gather_pair(after(shards[2], own_units_0)))
    near_attn_1 = gather_near(after(own_attn_1, near_attn_0))
    own_units_1 = gather_planes(gather_pair(after(shards[3], own_attn_1)))
    near_units_1 = gather_near(after(own_units_1, near_units_0))
    far_units_0 = gather_far(gather_halves(near_units_0))
    far_attn_1 = gather_far(gather_halves(near_attn_1))
    far_units_1 = gather_far(gather_halves(near_units_1))

    cond_float = cond.astype(wide)
    gated_low = jax.nn.silu(cond_float).astype(low)
    gated_own = lax.dynamic_slice_in_dim(gated_low, own_start, own_width, 1).astype(wide)
    w_ada_wide = w_ada.astype(wide)
    partial_mod = jnp.stack(
        [
            jnp.sum(gated_own[clip][None, :, None, None] * w_ada_wide, axis=1)
            for clip in range(clip_count)
        ],
        axis=1,
    )
    own_mod = jnp.sum(deal(sum_to_owner(partial_mod, all_devices)), axis=0).reshape(
        2, clip_count, 6, own_width
    )
    own_mod = own_mod + b_ada.astype(wide)[:, None]
    pieces = (own_mod, b_proj.astype(wide), b_fc1.astype(wide))
    packed = jnp.concatenate([piece.reshape(-1) for piece in pieces])
    dealt = deal(jnp.broadcast_to(packed[None], (all_devices, packed.shape[0])))
    first_end, second_end = pieces[0].size, pieces[0].size + pieces[1].size
    modulation = from_owners(dealt[:, :first_end], (2, clip_count, 6))
    proj_full = from_owners(dealt[:, first_end:second_end], (2, 4))
    hidden_full = from_owners(dealt[:, second_end:], (2,))

    frames_dev, place_half = tokens.shape[0], tokens.shape[2]
    frame_ids = lax.axis_index("dp") * frames_dev + jnp.arange(frames_dev, dtype=jnp.int32)
    onehot = (
        frame_ids[:, None] // FRAMES == jnp.arange(clip_count, dtype=jnp.int32)[None, :]
    ).astype(wide)
    first_mod = jnp.sum(onehot[:, :, None, None] * modulation[0][None], axis=1)
    second_mod = modulation[1]

    def layer_biases(layer):
        bias_query = tensor_part(proj_full[layer, 0])
        bias_value = tensor_part(proj_full[layer, 1])
        joined = jnp.concatenate([bias_query, jnp.zeros_like(bias_query), bias_value])
        return (
            jnp.pad(joined, (0, padded(joined_width) - joined_width))[None],
            proj_full[layer, 2:3],
            proj_full[layer, 3:4],
            lax.dynamic_slice_in_dim(hidden_full[layer], unit_start(units), units)[None],
        )

    def flat(values):
        return both_halves(values).reshape(-1, width)

    def own_places(values, frames):
        split = values.reshape(frames, 2, -1, width)
        return lax.dynamic_slice_in_dim(split, tensor, 1, 1)

    all_frames, own_place_count = frames_dev * dp_count, 2 * (place_half // dp_count)
    mods_0, mods_1 = first_mod, second_mod
    biases_0, biases_1 = layer_biases(0), layer_biases(1)

    upstream_1 = flat(out_grad)
    mlp_grad_1, turn_sums_1 = turn(upstream_1, mods_1)
    flat_grad_1 = pair_rows(mlp_grad_1)

    wattn_0 = arrange(*after((*near_attn_0, *far_attn_0), own_attn_1))
    x_0 = flat(tokens)
    hidden_0, joined_0, attended_0, both_0, middle_0, hidden_mlp = first_half(
        x_0, mods_0, wattn_0, biases_0, None
    )
    flat_0 = pair_rows(hidden_mlp)
    units_0 = arrange(*near_units_0, *far_units_0)
    slope_0, active_0, keep, send = units_forward(
        after(flat_0, near_attn_1, flat_grad_1), units_0, biases_0[3]
    )
    branch_0 = pair_sum(chip_sum(keep, send))
    result_0 = own_places(
        block_result(after(middle_0, near_units_1), branch_0, biases_0, mods_0), frames_dev
    )
    x_1 = flat(lax.all_to_all(result_0, "dp", split_axis=2, concat_axis=0, tiled=True))

    wattn_1 = arrange(*near_attn_1, *far_attn_1)
    hidden_1, joined_1, attended_1, both_1, middle_1, hidden_mlp = first_half(
        x_1, mods_1, wattn_1, biases_1, own_place_count
    )
    flat_1 = pair_rows(hidden_mlp)
    units_1 = arrange(*near_units_1, *far_units_1)
    slope_1, active_1, keep_1, send_1 = units_forward(flat_1, units_1, biases_1[3])

    inner_grad_1, keep, send, fc1_bias_1 = units_backward(flat_grad_1, units_1, slope_1)
    chip = chip_sum(keep, send)
    hidden_grad = pair_sum(chip)
    sums_units_1 = scatter_start(
        weight_grad(after(((flat_1, inner_grad_1), (flat_grad_1, active_1)), chip))
    )
    middle_grad, attn_grad, middle_sums_1 = middle_back(
        upstream_1, hidden_grad, middle_1, both_1, biases_1, mods_1
    )
    joined_grad, mine_grad, joined_bias_1 = attention_backward(
        attn_grad, wattn_1, joined_1, mods_1.shape[0], own_place_count
    )
    x_grad_1, input_sums_1 = input_back(middle_grad, mine_grad, x_1, mods_1, low)
    sent_back = own_places(x_grad_1, all_frames)
    arrived_back = lax.all_to_all(sent_back, "dp", split_axis=0, concat_axis=2, tiled=True)
    sums_attn_1 = scatter_start(
        weight_grad(after(((hidden_1, joined_grad), (attn_grad, attended_1)), sent_back))
    )
    sums_units_1 = scatter_near(after(sums_units_1, sums_attn_1[0]))

    branch_1 = pair_sum(chip_sum(*after((keep_1, send_1), attn_grad)))
    output = own_places(block_result(middle_1, branch_1, biases_1, mods_1), all_frames)
    gate_1 = gate_sums(upstream_1, branch_1, biases_1, mods_1)

    upstream_0 = flat(arrived_back)
    mlp_grad_0, turn_sums_0 = turn(upstream_0, mods_0)
    flat_grad_0 = pair_rows(mlp_grad_0)
    inner_grad_0, keep, send, fc1_bias_0 = units_backward(flat_grad_0, units_0, slope_0)
    chip = chip_sum(keep, send)
    hidden_grad = pair_sum(chip)
    sums_units_1, sums_attn_1, chip = together(sums_units_1, sums_attn_1, chip)
    sums_attn_1 = scatter_near(sums_attn_1)
    units_blocks = scatter_plane_blocks(sums_units_1)
    inner_grad_0 = after(inner_grad_0, chip, units_blocks)
    sums_units_1 = scatter_halve(units_blocks)
    sums_units_0 = scatter_start(weight_grad(((flat_0, inner_grad_0), (flat_grad_0, active_0))))
    middle_grad, attn_grad, middle_sums_0 = middle_back(
        upstream_0, hidden_grad, middle_0, both_0, biases_0, mods_0
    )
    sums_attn_1, sums_units_1, attn_grad = together(sums_attn_1, sums_units_1, attn_grad)
    sums_attn_1 = scatter_halve(scatter_plane_blocks(sums_attn_1))
    sums_units_1 = scatter_last(sums_units_1)
    joined_grad, mine_grad, joined_bias_0 = attention_backward(
        attn_grad, wattn_0, joined_0, mods_0.shape[0], None
    )
    sums_units_0, joined_grad = together(sums_units_0, joined_grad)
    sums_units_0 = scatter_near(sums_units_0)
    sums_attn_0 = scatter_start(weight_grad(((hidden_0, joined_grad), (attn_grad, attended_0))))
    x_grad_0, input_sums_0 = input_back(middle_grad, mine_grad, x_0, mods_0, wide)
    tokens_grad = own_places(x_grad_0, frames_dev)
    gate_0 = gate_sums(upstream_0, branch_0, biases_0, mods_0)
    sums_units_0, sums_attn_1, sums_units_1, input_sums_0, gate_0 = together(
        sums_units_0, sums_attn_1, sums_units_1, input_sums_0, gate_0
    )
    units_blocks = scatter_plane_blocks(sums_units_0)
    sums_units_0 = scatter_halve(units_blocks)
    sums_attn_1 = scatter_last(sums_attn_1)
    second_units = scatter_join(sums_units_1, True)
    mod_0, proj_0, hidden_bias_0 = small_grads(
        input_sums_0, middle_sums_0, gate_0, turn_sums_0, joined_bias_0, fc1_bias_0
    )
    mod_1, proj_1, hidden_bias_1 = small_grads(
        input_sums_1, middle_sums_1, gate_1, turn_sums_1, joined_bias_1, fc1_bias_1
    )
    clips_0 = jnp.sum(onehot[:, :, None, None] * mod_0[:, None], axis=0)
    small = (
        jnp.stack([clips_0, mod_1]),
        jnp.stack([proj_0, proj_1]),
        jnp.stack([hidden_bias_0, hidden_bias_1]),
    )
    dealt = jnp.concatenate([sum_to_owner(piece, all_devices) for piece in small], axis=1)
    owned = jnp.sum(deal(dealt), axis=0)
    sums_attn_0 = scatter_near(after(sums_attn_0, units_blocks, owned))
    own_dmod = owned[:first_end]
    b_proj_grad = owned[first_end:second_end].reshape(2, 4, own_width)
    b_fc1_grad = owned[second_end:].reshape(2, -1)
    summed_mod = from_owners(
        deal(jnp.broadcast_to(own_dmod[None], (all_devices, own_dmod.shape[0]))), (2, clip_count, 6)
    )
    sums_units_0, sums_attn_1, sums_attn_0, summed_mod = together(
        sums_units_0, sums_attn_1, sums_attn_0, summed_mod
    )
    second_attn = scatter_join(sums_attn_1)[0]
    sums_attn_0 = scatter_planes(sums_attn_0)
    sums_units_0 = scatter_last(sums_units_0)
    first_units = scatter_join(sums_units_0, True)
    first_attn = scatter_finish(sums_attn_0)
    w_ada_grad = sum(
        gated_own[clip][None, :, None, None] * summed_mod[:, clip][:, None]
        for clip in range(clip_count)
    )
    b_ada_grad = jnp.sum(own_dmod.reshape(2, clip_count, 6, own_width), axis=1)
    silu_grad = jnp.stack(
        [
            jnp.sum(summed_mod[:, clip][:, None] * w_ada_wide, axis=(0, 2, 3))
            for clip in range(clip_count)
        ]
    )
    cond_own = lax.dynamic_slice_in_dim(cond_float, own_start, own_width, 1)
    cond_grad = jax.vjp(jax.nn.silu, cond_own)[1](silu_grad)[0]

    reduced = ((first_attn, first_units), (second_attn, second_units))
    out_start = padded(joined_width)
    w_qkv_grad = jnp.stack(
        [part[0][:, :joined_width].reshape(own_rows, 3, head_width) for part in reduced]
    )
    w_out_grad = jnp.stack(
        [part[0][:, out_start : out_start + head_width].T for part in reduced]
    )
    w_fc1_grad = jnp.stack(
        [jnp.concatenate([part[1][0, :, :units], part[1][1, :, :units]], axis=1) for part in reduced]
    )
    w_fc2_grad = jnp.stack(
        [part[1][:, :, units:].transpose(0, 2, 1).reshape(2 * units, own_rows) for part in reduced]
    )
    return (
        output,
        tokens_grad,
        cond_grad,
        w_qkv_grad,
        w_out_grad,
        w_fc1_grad,
        w_fc2_grad,
        w_ada_grad,
        b_ada_grad,
        b_proj_grad,
        b_fc1_grad,
    )


def solution(mesh):
    return jax.shard_map(
        per_device,
        mesh=mesh,
        in_specs=(
            P("dp", "tensor", None, None),
            P(),
            P(None, "tensor", "dp", None),
            P(None, "dp", None, "tensor"),
            P(None, "tensor", "dp"),
            P(None, "dp", "tensor"),
            P(None, "tensor", "dp"),
            P(None, ("dp", "tensor"), None, None),
            P(None, None, ("dp", "tensor")),
            P(None, None, ("dp", "tensor")),
            P(None, ("dp", "tensor")),
        ),
        out_specs=(
            P(None, "tensor", "dp", None),
            P("dp", "tensor", None, None),
            P(None, ("dp", "tensor")),
            P(None, "dp", None, "tensor"),
            P(None, "tensor", "dp"),
            P(None, "dp", "tensor"),
            P(None, "tensor", "dp"),
            P(None, ("dp", "tensor"), None, None),
            P(None, None, ("dp", "tensor")),
            P(None, None, ("dp", "tensor")),
            P(None, ("dp", "tensor")),
        ),
        check_vma=False,
    )
```

```python
import functools

import jax
import jax.numpy as jnp
from jax import lax
from jax.experimental import pallas as pl
from jax.experimental.pallas import tpu as pltpu
from jax.sharding import PartitionSpec as P

HEAD_DIM = 72
FRAMES = 16


epsilon = 1e-06
highest = lax.Precision.HIGHEST
low = jnp.bfloat16
wide = jnp.float32
everyone = ("dp", "tensor")


def layer_norm(values):
    centred = values - jnp.mean(values, axis=-1, keepdims=True)
    inverse = lax.rsqrt(jnp.mean(centred * centred, axis=-1, keepdims=True) + epsilon)
    return (centred * inverse, inverse)


def layer_norm_back(normed, inverse, upstream):
    first_moment = jnp.mean(upstream, axis=-1, keepdims=True)
    second_moment = jnp.mean(upstream * normed, axis=-1, keepdims=True)
    return inverse * (upstream - first_moment - normed * second_moment)


def product(left_side, right_side):
    return jnp.dot(left_side, right_side, preferred_element_type=wide)


def product_left(left_side, right_side):
    return lax.dot_general(
        left_side, right_side, (((0,), (0,)), ((), ())), preferred_element_type=wide
    )


def product_right(left_side, right_side):
    return lax.dot_general(
        left_side, right_side, (((1,), (1,)), ((), ())), preferred_element_type=wide
    )


PAIR = 2


def swap_by(values, offset):
    count = lax.axis_size("dp")
    return lax.ppermute(values, "dp", [(i, i ^ offset) for i in range(count)])


def my_bit(bit):
    return (lax.axis_index("dp") >> bit) & 1


def after(values, *others):
    return lax.optimization_barrier((values,) + others)[0]


def pick(first, mine, theirs, axis):
    return jnp.stack(
        [jnp.where(first, mine, theirs), jnp.where(first, theirs, mine)], axis=axis
    )


def place_scalars():
    return jnp.stack(
        [lax.axis_index("tensor"), lax.axis_index("dp") & 3, lax.axis_index("dp") >> 2]
    ).astype(jnp.int32)


def gather_pair(shard):
    paired = isinstance(shard, tuple)
    own, sent = shard if paired else (shard, shard)
    return jnp.stack([own, swap_by(sent, 1 << PAIR)])


def gather_planes(held):
    while held.shape[0] * 4 < lax.axis_size("dp"):
        held = jnp.concatenate([held, swap_by(held, held.shape[0] * 4)])
    return held


def gather_straight(shard):
    paired = isinstance(shard, tuple)
    parts = [shard[0] if paired else shard]
    for relative in range(1, lax.axis_size("dp") // 4):
        sent = shard[relative & 1] if paired else shard
        parts.append(swap_by(sent, relative << 2))
    return jnp.stack(parts)


def arrange_kernel(place_ref, own_ref, across_ref, along_ref, low_ref, high_ref, out_ref):
    me = place_ref[1]
    out_ref[me] = own_ref[0]
    out_ref[me ^ 1] = across_ref[0]
    out_ref[me ^ 2] = along_ref[0]
    in_low = pl.program_id(0) < pl.num_programs(0) // 2

    @pl.when(in_low)
    def _():
        out_ref[me ^ 3] = low_ref[0]

    @pl.when(jnp.logical_not(in_low))
    def _():
        out_ref[me ^ 3] = high_ref[0]


def arrange(own, across, along, low_part, high_part):
    groups, rows, columns = own.shape
    half = groups // 2
    block = (1, rows, columns)
    whole = pl.BlockSpec(block, lambda i, place: (i, 0, 0))
    out = pl.pallas_call(
        arrange_kernel,
        out_shape=jax.ShapeDtypeStruct((groups * 4, rows, columns), own.dtype),
        grid_spec=pltpu.PrefetchScalarGridSpec(
            num_scalar_prefetch=1,
            grid=(groups,),
            in_specs=[
                whole,
                whole,
                whole,
                pl.BlockSpec(block, lambda i, place: (jnp.minimum(i, half - 1), 0, 0)),
                pl.BlockSpec(block, lambda i, place: (jnp.maximum(i - half, 0), 0, 0)),
            ],
            out_specs=pl.BlockSpec((4, rows, columns), lambda i, place: (i ^ place[2], 0, 0)),
        ),
        name="arrange",
        cost_estimate=cost(0, 16 * groups * rows * columns),
    )(place_scalars(), own, across, along, low_part, high_part)
    return out.reshape(groups * 4 * rows, columns)


def gather_near(own):
    return (own, swap_by(own, 1), swap_by(own, 2))


def gather_halves(near):
    half = near[0].shape[0] // 2
    return (near[1][:half], near[2][half:])


def gather_far(halves):
    return (swap_by(halves[0], 2), swap_by(halves[1], 1))


def weight_grad_kernel(count, starts, lefts, place_ref, *refs):
    pairs = len(starts)
    operands, outs = refs[: pairs * (lefts + 1)], refs[pairs * (lefts + 1) : -2]
    left_rows, total = refs[-2:]
    own, to_across, to_along, rest_across, rest_along = outs
    me, plane = place_ref[1], place_ref[2]
    rows, groups = total.shape[0] // count, count // 4
    half = groups // 2
    for index, start in enumerate(starts):
        *parts, right = operands[index * (lefts + 1) : (index + 1) * (lefts + 1)]
        if lefts == 1:
            left = parts[0][...]
        else:
            for at, part in enumerate(parts):
                left_rows[at * part.shape[0] : (at + 1) * part.shape[0]] = part[...]
            left = left_rows[...]
        total[:, start : start + right.shape[1]] = product_left(left, right[...])
        spare = -right.shape[1] % 128
        if spare:
            end = start + right.shape[1]
            total[:, end : end + spare] = jnp.zeros((total.shape[0], spare), wide)

    def copy(out, at, mate, first, length):
        place = me ^ mate
        if rows % 8 == 0:

            @pl.loop(0, length)
            def _(step):
                chip = (plane ^ (first + step)) * 4 + place
                out[at + step] = total[pl.ds(pl.multiple_of(chip * rows, 8), rows), :].astype(low)

        else:

            for chip in range(count):

                @pl.when((chip & 3) == place)
                def _(chip=chip):
                    step = (plane ^ (chip >> 2)) - first

                    @pl.when((step >= 0) & (step < length))
                    def _():
                        out[at + step] = total[chip * rows : (chip + 1) * rows, :].astype(low)

    copy(to_along, 0, 3, 0, half)
    copy(to_along, half, 2, 0, half)
    copy(to_across, 0, 3, half, half)
    copy(to_across, half, 1, half, half)
    copy(rest_across, 0, 1, 0, half)
    copy(rest_along, 0, 2, half, half)
    copy(own, 0, 0, 0, groups)


def weight_grad(pairs):
    count = lax.axis_size("dp")
    groups = count // 4
    half = groups // 2
    lefts = len(pairs[0][0])
    width = pairs[0][0][0].shape[1]
    rows = width // count
    starts, columns = [], 0
    for _, right in pairs:
        starts.append(columns)
        columns += padded(right.shape[1])
    tokens = pairs[0][1].shape[0]
    own, to_across, to_along, rest_across, rest_along = pl.pallas_call(
        functools.partial(weight_grad_kernel, count, tuple(starts), lefts),
        out_shape=[
            jax.ShapeDtypeStruct((blocks, rows, columns), low)
            for blocks in (groups, groups, groups, half, half)
        ],
        in_specs=[pl.BlockSpec(memory_space=pltpu.SMEM)]
        + [pl.BlockSpec(memory_space=pltpu.VMEM)] * ((lefts + 1) * len(pairs)),
        scratch_shapes=[pltpu.VMEM((tokens, width), low), pltpu.VMEM((width, columns), wide)],
        name="weight_grad",
        cost_estimate=cost(
            2 * tokens * width * columns, 2 * width * columns + 4 * tokens * (width + columns)
        ),
    )(place_scalars(), *[operand for left, right in pairs for operand in (*left, right)])
    return (own, rest_across, rest_along, to_across, to_along)


def scatter_start(parts):
    own, rest_across, rest_along, to_across, to_along = parts
    return (own, rest_across, rest_along, swap_by(to_across, 1), swap_by(to_along, 2))


def scatter_near_sums(state):
    own, rest_across, rest_along, got_across, got_along = state
    half = rest_across.shape[0]
    rest_across = (rest_across.astype(wide) + got_along[:half].astype(wide)).astype(low)
    rest_along = (rest_along.astype(wide) + got_across[:half].astype(wide)).astype(low)
    return (own, got_across, got_along, rest_across, rest_along)


def scatter_near(sums):
    own, got_across, got_along, rest_across, rest_along = sums
    return (own, got_across, got_along, swap_by(rest_across, 1), swap_by(rest_along, 2))


def scatter_plane_blocks(state):
    own, got_across, got_along, last_across, last_along = state
    half = own.shape[0] // 2

    def total(relative):
        block = own[relative].astype(wide)
        if relative < half:
            return block + got_along[half + relative].astype(wide) + last_across[relative].astype(wide)
        return block + got_across[relative].astype(wide) + last_along[relative - half].astype(wide)

    return [total(relative) for relative in range(own.shape[0])]


def scatter_planes(blocks):
    got = [
        swap_by(block.astype(low), relative << 2) for relative, block in enumerate(blocks) if relative
    ]
    return (blocks[0], got)


def scatter_finish(state):
    own, got = state
    return own + sum(part.astype(wide) for part in got)


def scatter_halve(blocks):
    half = len(blocks) // 2
    sent = jnp.stack([block.astype(low) for block in blocks[half:]])
    return (blocks[:half], swap_by(sent, half * 4))


def scatter_join(state, paired=False):
    kept, got = state
    if paired:
        return pick(my_bit(PAIR) == 0, kept[0], got[0].astype(wide), 0)
    return [block + got[index].astype(wide) for index, block in enumerate(kept)]


def scatter_last(state):
    blocks = scatter_join(state)
    while len(blocks) > 2:
        blocks = scatter_join(scatter_halve(blocks))
    return scatter_halve(blocks)


def swap_tensor(values):
    return lax.ppermute(values, "tensor", [(0, 1), (1, 0)])


def both_halves(values):
    return lax.all_gather(values, "tensor", axis=1, tiled=True)


def own_half(values):
    return lax.dynamic_slice_in_dim(
        values, lax.axis_index("tensor") * (values.shape[1] // 2), values.shape[1] // 2, 1
    )


def pair_part(values):
    half = values.shape[0] // 2
    return lax.dynamic_slice_in_dim(values, lax.axis_index("tensor") * half, half, 0)


def pair_rows(values, sent):
    got = swap_by(sent, 1 << PAIR)
    return (values, lax.all_gather(got, "tensor", axis=0, tiled=True))


def chip_sum(keep, send):
    return keep.astype(wide) + swap_tensor(send).astype(wide)


def pair_sum(chip):
    got = swap_by(chip[1].astype(low), 1 << PAIR)
    total = (chip[0] + got.astype(wide)).astype(low)
    return lax.all_gather(total, "tensor", axis=0, tiled=True)


def unit_start(units):
    return (lax.axis_index("tensor") * 2 + my_bit(PAIR)) * units


def deal(values):
    return lax.all_to_all(values, everyone, split_axis=0, concat_axis=0, tiled=True)


def sum_to_owner(values, owners):
    lead = values.shape[:-1]
    dealt = jnp.moveaxis(values.reshape(lead + (owners, -1)), -2, 0)
    return dealt.reshape(owners, -1)


def from_owners(values, lead):
    owners = values.shape[0]
    return jnp.moveaxis(values.reshape((owners,) + lead + (-1,)), 0, -2).reshape(lead + (-1,))


def padded(width):
    return width + -width % 128


def fixed(*shape):
    return pl.BlockSpec(shape, lambda i, *_: (0,) * len(shape))


def by_rows(rows, *rest):
    return pl.BlockSpec((rows,) + rest, lambda i, *_: (i,) + (0,) * len(rest))


COST_SHARE = 16


def by_group(*rest):
    return pl.BlockSpec((1,) + rest, lambda i, *_: (i // STEPS,) + (0,) * len(rest))


def cost(flops, bytes_accessed, transcendentals=0):
    return pl.CostEstimate(
        flops=flops // COST_SHARE,
        bytes_accessed=bytes_accessed // COST_SHARE,
        transcendentals=transcendentals // COST_SHARE,
    )


STEPS = 2


def add_sums(sums_ref, *values):
    @pl.when(lax.rem(pl.program_id(0), STEPS) == 0)
    def _():
        sums_ref[...] = jnp.zeros_like(sums_ref)

    for row, value in enumerate(values):
        sums_ref[0, row : row + 1] += column_sum(value)


def column_sum(values):
    return jnp.sum(values, axis=0, keepdims=True)


def same_place(rows, place_count):
    if rows == place_count:
        return None
    first = lax.broadcasted_iota(jnp.int32, (rows, rows), 0)
    second = lax.broadcasted_iota(jnp.int32, (rows, rows), 1)
    return lax.rem(first, place_count) == lax.rem(second, place_count)


def head_probs(query, keys, mask):
    scores = product_right(query, keys) * (HEAD_DIM ** (-0.5))
    if mask is not None:
        scores = jnp.where(mask, scores, -1e30)
    exponent = jnp.exp(scores - jnp.max(scores, axis=-1, keepdims=True))
    return exponent * (1.0 / jnp.sum(exponent, axis=-1, keepdims=True))


def attention_kernel(
    place_count, x_ref, mod_ref, weight_ref, bias_ref, hidden_ref, joined_ref, attended_ref, out_ref
):
    rows, width = attended_ref.shape
    joined_width = joined_ref.shape[1]
    normed, _ = layer_norm(x_ref[...].astype(wide))
    hidden = (normed * (1.0 + mod_ref[0, 1:2]) + mod_ref[0, 0:1]).astype(low)
    hidden_ref[...] = hidden
    joined_ref[...] = (product(hidden, weight_ref[:, :joined_width]) + bias_ref[...]).astype(low)
    mask = None if place_count is None else same_place(rows, place_count)
    for start in range(0, width, HEAD_DIM):
        query, keys, value = (
            joined_ref[:, part * width + start : part * width + start + HEAD_DIM]
            for part in range(3)
        )
        probs = head_probs(query, keys, mask).astype(low)
        attended_ref[:, start : start + HEAD_DIM] = product(probs, value).astype(low)
    out_ref[...] = product_right(
        attended_ref[...], weight_ref[:, joined_width : joined_width + width]
    ).astype(low)


def attention_back_kernel(
    place_count, upstream_ref, weight_ref, joined_ref, grad_ref, out_ref, bias_ref
):
    rows, joined_width = joined_ref.shape
    width = upstream_ref.shape[1] // 2
    score_scale = HEAD_DIM ** (-0.5)
    attended_grad = product(
        upstream_ref[...], weight_ref[:, joined_width : joined_width + width]
    ).astype(low)
    mask = None if place_count is None else same_place(rows, place_count)
    for start in range(0, width, HEAD_DIM):
        query, keys, value = (
            joined_ref[:, part * width + start : part * width + start + HEAD_DIM]
            for part in range(3)
        )
        upstream = attended_grad[:, start : start + HEAD_DIM]
        scores = product_right(keys, query) * score_scale
        if mask is not None:
            scores = jnp.where(mask, scores, -1e30)
        exponent = jnp.exp(scores - jnp.max(scores, axis=0, keepdims=True))
        probs = exponent * (1.0 / jnp.sum(exponent, axis=0, keepdims=True))
        value_grad = product(probs.astype(low), upstream)
        prob_grad = product_right(value, upstream)
        centre = jnp.sum(probs * prob_grad, axis=0, keepdims=True)
        score_grad = (probs * (prob_grad - centre)).astype(low)
        query_grad = product_left(score_grad, keys) * score_scale
        keys_grad = product(score_grad, query) * score_scale
        for part, grad in enumerate((query_grad, keys_grad, value_grad)):
            grad_ref[:, part * width + start : part * width + start + HEAD_DIM] = grad.astype(low)
    spare = joined_width - 3 * width
    if spare:
        grad_ref[:, 3 * width :] = jnp.zeros((rows, spare), low)
    joined_grad = grad_ref[...]
    bias_ref[0] = column_sum(joined_grad.astype(wide))
    out_ref[...] = product_right(joined_grad, weight_ref[:, :joined_width]).astype(low)


def middle_kernel(x_ref, mine_ref, theirs_ref, bias_ref, mod_ref, middle_ref, hidden_ref):
    branch = mine_ref[...].astype(wide) + theirs_ref[...].astype(wide) + bias_ref[...]
    middle = x_ref[...].astype(wide) + mod_ref[0, 2:3] * branch
    middle_ref[...] = middle
    normed, _ = layer_norm(middle)
    hidden_ref[...] = (normed * (1.0 + mod_ref[0, 4:5]) + mod_ref[0, 3:4]).astype(low)


def split_halves(place_ref, partial_ref, keep_ref, send_ref):
    tensor = place_ref[0]
    half = keep_ref.shape[1]
    keep_ref[0] = partial_ref[pl.ds(pl.multiple_of(tensor * half, 8), half), :].astype(low)
    send_ref[0] = partial_ref[pl.ds(pl.multiple_of((1 - tensor) * half, 8), half), :].astype(low)


def gelu_parts(values):
    root = 0.7978845608028654
    square = values * values
    bend = jnp.tanh(root * (values + 0.044715 * values * square))
    share = 0.5 * (1.0 + bend)
    steep = 0.5 * root * (1.0 - bend * bend) * (1.0 + 3.0 * 0.044715 * square)
    return (values * share, share + values * steep)


def units_kernel(
    place_ref,
    own_ref,
    other_ref,
    up_ref,
    down_ref,
    bias_ref,
    slope_ref,
    active_ref,
    keep_ref,
    send_ref,
    partial_ref,
):
    hidden = jnp.where(pl.program_id(0) == 0, own_ref[...], other_ref[...])
    inner = product(hidden, up_ref[...]) + bias_ref[...]
    active, slope = gelu_parts(inner)
    slope_ref[...] = slope.astype(low)
    active = active.astype(low)
    active_ref[...] = active
    partial_ref[...] = product_right(active, down_ref[...])
    split_halves(place_ref, partial_ref, keep_ref, send_ref)


def units_back_kernel(
    place_ref,
    own_ref,
    other_ref,
    up_ref,
    down_ref,
    slope_ref,
    grad_ref,
    keep_ref,
    send_ref,
    bias_ref,
    partial_ref,
):
    upstream = jnp.where(pl.program_id(0) == 0, own_ref[...], other_ref[...])
    grad = (product(upstream, down_ref[...]) * slope_ref[...].astype(wide)).astype(low)
    grad_ref[...] = grad

    @pl.when(pl.program_id(0) == 0)
    def _():
        bias_ref[...] = jnp.zeros_like(bias_ref)

    bias_ref[...] += column_sum(grad.astype(wide))
    partial_ref[...] = product_right(grad, up_ref[...])
    split_halves(place_ref, partial_ref, keep_ref, send_ref)


def result_kernel(middle_ref, branch_ref, bias_ref, mod_ref, out_ref):
    branch = branch_ref[...].astype(wide) + bias_ref[...]
    out_ref[...] = (middle_ref[...] + mod_ref[0, 5:6] * branch).astype(low)


def turn_kernel(upstream_ref, mod_ref, grad_ref, sums_ref):
    grad = (upstream_ref[...].astype(wide) * mod_ref[0, 5:6]).astype(low)
    grad_ref[...] = grad
    add_sums(sums_ref, grad.astype(wide))


def gate_kernel(upstream_ref, branch_ref, bias_ref, mod_ref, sums_ref):
    branch = branch_ref[...].astype(wide) + bias_ref[...]
    add_sums(sums_ref, upstream_ref[...].astype(wide) * branch)


def middle_back_kernel(
    upstream_ref,
    hidden_ref,
    middle_ref,
    mine_ref,
    theirs_ref,
    bias_ref,
    mod_ref,
    out_ref,
    grad_ref,
    sums_ref,
):
    normed, inverse = layer_norm(middle_ref[...])
    hidden_grad = hidden_ref[...].astype(wide)
    middle_grad = upstream_ref[...].astype(wide) + layer_norm_back(
        normed, inverse, hidden_grad * (1.0 + mod_ref[0, 4:5])
    )
    out_ref[...] = middle_grad
    grad = (middle_grad * mod_ref[0, 2:3]).astype(low)
    grad_ref[...] = grad
    branch = mine_ref[...].astype(wide) + theirs_ref[...].astype(wide) + bias_ref[...]
    add_sums(
        sums_ref, hidden_grad, hidden_grad * normed, middle_grad * branch, grad.astype(wide)
    )


def input_back_kernel(middle_ref, mine_ref, theirs_ref, x_ref, mod_ref, out_ref, sums_ref):
    normed, inverse = layer_norm(x_ref[...].astype(wide))
    hidden_grad = mine_ref[...].astype(wide) + theirs_ref[...].astype(wide)
    out_ref[...] = (
        middle_ref[...] + layer_norm_back(normed, inverse, hidden_grad * (1.0 + mod_ref[0, 1:2]))
    ).astype(out_ref.dtype)
    add_sums(sums_ref, hidden_grad, hidden_grad * normed)


def array(dtype, *shape):
    return jax.ShapeDtypeStruct(shape, dtype)


def attention_forward(x, mods, weight, bias, place_count):
    rows, width = x.shape
    groups = mods.shape[0]
    block = rows // groups
    part, joined = width // 2, bias.shape[1]
    return pl.pallas_call(
        functools.partial(attention_kernel, place_count),
        grid=(groups,),
        in_specs=[
            by_rows(block, width),
            by_rows(1, 6, width),
            fixed(*weight.shape),
            fixed(*bias.shape),
        ],
        out_specs=[by_rows(block, n) for n in (width, joined, part, width)],
        out_shape=[array(low, rows, n) for n in (width, joined, part, width)],
        name="attention",
        cost_estimate=cost(
            2 * rows * width * (joined + part) + 4 * rows * block * part,
            2 * weight.size + 2 * rows * (3 * width + joined + part),
            rows * block * part // HEAD_DIM,
        ),
    )(x, mods, weight, bias)


def attention_backward(upstream, weight, joined, groups, place_count):
    rows, width = upstream.shape
    block = rows // groups
    columns = joined.shape[1]
    return pl.pallas_call(
        functools.partial(attention_back_kernel, place_count),
        grid=(groups,),
        in_specs=[by_rows(block, width), fixed(*weight.shape), by_rows(block, columns)],
        out_specs=[by_rows(block, columns), by_rows(block, width), by_rows(1, 1, columns)],
        out_shape=[
            array(low, rows, columns),
            array(low, rows, width),
            array(wide, groups, 1, columns),
        ],
        name="attention_back",
        cost_estimate=cost(
            2 * rows * width * weight.shape[1] + 5 * rows * block * width,
            2 * weight.size + 2 * rows * (2 * width + 2 * columns),
            rows * block * width // (2 * HEAD_DIM),
        ),
    )(upstream, weight, joined)


def row_kernel(body, groups, row_inputs, fixed_inputs, mods, outs, sums, name, sent=None):
    rows, width = row_inputs[0].shape
    block = rows // (groups * STEPS)
    sum_shape = [array(wide, groups, 8, width)] * sums
    moved = sum(item.size * item.dtype.itemsize for item in row_inputs)
    first_out = len(row_inputs) + len(fixed_inputs) + 1
    alone = sent is not None and groups == 1 and STEPS == 2

    def steps(place_ref, *refs):
        body(*refs[:-1])

        @pl.when(pl.program_id(0) == place_ref[0])
        def _():
            refs[-1][...] = refs[first_out + sent][...]

    results = pl.pallas_call(
        steps if alone else body,
        grid_spec=pltpu.PrefetchScalarGridSpec(
            num_scalar_prefetch=int(alone),
            grid=(groups * STEPS,),
            in_specs=[by_rows(block, width) for _ in row_inputs]
            + [fixed(*item.shape) for item in fixed_inputs]
            + [by_group(6, width)],
            out_specs=[by_rows(block, width) for _ in outs]
            + [by_group(8, width)] * sums
            + [fixed(block, width)] * alone,
        ),
        out_shape=[array(dtype, rows, width) for dtype in outs]
        + sum_shape
        + [array(low, block, width)] * alone,
        name=name,
        cost_estimate=cost(20 * rows * width, moved + 4 * rows * width * len(outs)),
    )(*[place_scalars()] * alone, *row_inputs, *fixed_inputs, mods)
    if sent is not None and not alone:
        results = [*results, pair_part(results[sent])]
    return results


def units_call(body, rows_in, updown, extra, extra_spec, outs, out_specs, name):
    half, width = rows_in[0].shape
    units = updown.shape[1] // 2
    rows = 2 * half
    halves = array(low, 2, half // 2, width)
    at = pl.BlockSpec((1, half // 2, width), lambda i, *_: (i, 0, 0))
    return pl.pallas_call(
        body,
        grid_spec=pltpu.PrefetchScalarGridSpec(
            num_scalar_prefetch=1,
            grid=(2,),
            in_specs=[
                fixed(half, width),
                fixed(half, width),
                pl.BlockSpec((width, units), lambda i, *_: (0, 0)),
                pl.BlockSpec((width, units), lambda i, *_: (0, 1)),
                extra_spec,
            ],
            out_specs=out_specs[: len(outs) - 1] + [at, at] + out_specs[len(outs) - 1 :]
            if name == "units_back"
            else out_specs + [at, at],
            scratch_shapes=[pltpu.VMEM((half, width), wide)],
        ),
        out_shape=outs[:-1] + [halves, halves] + outs[-1:]
        if name == "units_back"
        else outs + [halves, halves],
        name=name,
        cost_estimate=cost(
            4 * rows * width * units,
            4 * width * units + 4 * rows * width + 6 * rows * units,
            rows * units,
        ),
    )(place_scalars(), *rows_in, updown, updown, extra)


def units_forward(hidden, updown, bias):
    rows, units = 2 * hidden[0].shape[0], updown.shape[1] // 2
    block = by_rows(rows // 2, units)
    return units_call(
        units_kernel,
        hidden,
        updown,
        bias,
        fixed(1, units),
        [array(low, rows, units), array(low, rows, units)],
        [block, block],
        "units",
    )


def units_backward(upstream, updown, slope):
    rows, units = slope.shape
    block = by_rows(rows // 2, units)
    return units_call(
        units_back_kernel,
        upstream,
        updown,
        slope,
        block,
        [array(low, rows, units), array(wide, 1, units)],
        [block, fixed(1, units)],
        "units_back",
    )


def first_half(x, mods, wattn, biases, place_count, *others):
    hidden, joined, attended, mine = attention_forward(x, mods, wattn, biases[0], place_count)
    both = after((mine, swap_tensor(mine)), *others)
    middle, hidden_mlp, sent = row_kernel(
        middle_kernel, mods.shape[0], (x, *both), (biases[1],), mods, (wide, low), 0, "middle", 1
    )
    return (hidden, joined, attended, both, middle, (hidden_mlp, sent))


def block_result(middle, branch, biases, mods):
    return row_kernel(
        result_kernel, mods.shape[0], (middle, branch), (biases[2],), mods, (low,), 0, "result"
    )[0]


def turn(upstream, mods):
    grad, sums, sent = row_kernel(
        turn_kernel, mods.shape[0], (upstream,), (), mods, (low,), 1, "turn", 0
    )
    return (grad, sent), sums


def gate_sums(upstream, branch, biases, mods):
    return row_kernel(
        gate_kernel, mods.shape[0], (upstream, branch), (biases[2],), mods, (), 1, "gate"
    )[0]


def middle_back(upstream, hidden_grad, middle, both, biases, mods):
    return row_kernel(
        middle_back_kernel,
        mods.shape[0],
        (upstream, hidden_grad, middle, *both),
        (biases[1],),
        mods,
        (wide, low),
        1,
        "middle_back",
    )


def input_back(middle_grad, mine_grad, x, mods, grad_dtype):
    return row_kernel(
        input_back_kernel,
        mods.shape[0],
        (middle_grad, mine_grad, swap_tensor(mine_grad), x),
        (),
        mods,
        (grad_dtype,),
        1,
        "input_back",
    )


def pack_kernel(clips, scalars_ref, *refs):
    out = refs[-1]
    tensor, pair, first_frame = scalars_ref[0], scalars_ref[1], scalars_ref[2]
    out[...] = jnp.zeros_like(out)
    per_block = out.shape[0] // 2
    width = out.shape[1]
    for block in range(2):
        inputs, middles, gate, turned, joined, fc1 = refs[6 * block : 6 * block + 6]
        base = block * per_block
        for group in range(gate.shape[0]):
            clip = group if block else lax.div(first_frame + group, FRAMES)
            if clips == 1:
                clip = 0
            parts = (
                (inputs, 0), (inputs, 1), (middles, 2), (middles, 0), (middles, 1), (gate, 0)
            )
            for index, (ref, row) in enumerate(parts):
                out[pl.ds(base + clip * 6 + index, 1), :] += 0.5 * ref[group, row : row + 1]
            place = base + clips * 6
            out[place : place + 1, :] += 0.5 * middles[group, 3:4]
            out[place + 1 : place + 2, :] += 0.5 * turned[group, 0:1]
            at = place + 2 + 2 * tensor
            spare = joined.shape[2] - width
            out[pl.ds(at, 1), :] += joined[group, :, :width]
            out[pl.ds(at + 1, 1), :spare] += joined[group, :, width:]
        out[pl.ds(base + clips * 6 + 6 + 2 * tensor + pair, 1), :] += fc1[...]


def pack_sums(clips, first_frame, blocks):
    width = blocks[0][0].shape[2]
    rows = 2 * (6 * clips + 10)
    scalars = jnp.stack([lax.axis_index("tensor"), my_bit(PAIR), first_frame]).astype(jnp.int32)
    operands = [item for block in blocks for item in block]
    return pl.pallas_call(
        functools.partial(pack_kernel, clips),
        out_shape=array(wide, rows, width),
        in_specs=[pl.BlockSpec(memory_space=pltpu.SMEM)]
        + [pl.BlockSpec(memory_space=pltpu.VMEM)] * len(operands),
        name="pack",
        cost_estimate=cost(rows * width, 8 * rows * width),
    )(scalars, *operands)


def tensor_part(values):
    part = values.shape[-1] // 2
    return lax.dynamic_slice_in_dim(
        values, lax.axis_index("tensor") * part, part, values.ndim - 1
    )


def per_device(tokens, cond, out_grad, w_qkv, w_out, w_fc1, w_fc2, w_ada, b_ada, b_proj, b_fc1):
    dp_count = lax.axis_size("dp")
    all_devices = lax.axis_size(everyone)
    flat_index = lax.axis_index(everyone)
    tensor = lax.axis_index("tensor")
    width = tokens.shape[3]
    clip_count = cond.shape[0]
    own_rows, head_width = w_qkv.shape[1], w_qkv.shape[3]
    units = w_fc1.shape[2] // 2
    own_width = width // all_devices
    own_start = flat_index * own_width
    joined_width = 3 * head_width

    def pad_columns(values):
        return jnp.pad(values, ((0, 0), (0, padded(values.shape[1]) - values.shape[1])))

    def units_part(layer, side):
        first = side * units
        return jnp.concatenate(
            [
                lax.dynamic_slice_in_dim(w_fc1[layer], first, units, 1),
                lax.dynamic_slice_in_dim(w_fc2[layer], first, units, 0).T,
            ],
            axis=1,
        )

    shards = []
    for layer in range(2):
        shards.append(
            jnp.concatenate(
                [
                    pad_columns(w_qkv[layer].reshape(own_rows, joined_width)),
                    pad_columns(w_out[layer].T),
                ],
                axis=1,
            )
        )
        shards.append((units_part(layer, my_bit(PAIR)), units_part(layer, 1 - my_bit(PAIR))))
    cond_float = cond.astype(wide)
    gated_low = jax.nn.silu(cond_float).astype(low)
    gated_own = lax.dynamic_slice_in_dim(gated_low, own_start, own_width, 1).astype(wide)
    w_ada_wide = w_ada.astype(wide)
    partial_mod = jnp.stack(
        [
            jnp.sum(gated_own[clip][None, :, None, None] * w_ada_wide, axis=1)
            for clip in range(clip_count)
        ],
        axis=1,
    )
    own_mod = jnp.sum(deal(sum_to_owner(partial_mod, all_devices)), axis=0).reshape(
        2, clip_count, 6, own_width
    )
    own_mod = own_mod + b_ada.astype(wide)[:, None]
    pieces = (own_mod, b_proj.astype(wide), b_fc1.astype(wide))
    packed = jnp.concatenate([piece.reshape(-1) for piece in pieces])
    dealt = deal(jnp.broadcast_to(packed[None], (all_devices, packed.shape[0])))

    own_attn_0 = gather_straight(shards[0])
    near_attn_0 = gather_near(after(own_attn_0, dealt))
    own_units_0 = gather_straight(after(shards[1], own_attn_0))
    pair_attn_1 = gather_pair(after(shards[2], own_attn_0, own_units_0, near_attn_0))
    pair_units_1 = gather_pair(after(shards[3], pair_attn_1))
    far_attn_0 = gather_far(gather_halves(near_attn_0))
    near_units_0 = gather_near(own_units_0)
    own_attn_1 = gather_planes(pair_attn_1)
    own_units_1 = gather_planes(after(pair_units_1, own_attn_1, near_units_0))
    near_attn_1 = gather_near(after(own_attn_1, near_attn_0, far_attn_0))
    far_units_0 = gather_far(gather_halves(near_units_0))
    near_units_1 = gather_near(after(own_units_1, near_units_0))
    far_attn_1 = gather_far(gather_halves(near_attn_1))
    far_units_1 = gather_far(gather_halves(near_units_1))
    dealt = after(dealt, near_units_0)
    first_end, second_end = pieces[0].size, pieces[0].size + pieces[1].size
    modulation = from_owners(dealt[:, :first_end], (2, clip_count, 6))
    proj_full = from_owners(dealt[:, first_end:second_end], (2, 4))
    hidden_full = from_owners(dealt[:, second_end:], (2,))

    frames_dev, place_half = tokens.shape[0], tokens.shape[2]
    frame_ids = lax.axis_index("dp") * frames_dev + jnp.arange(frames_dev, dtype=jnp.int32)
    onehot = (
        frame_ids[:, None] // FRAMES == jnp.arange(clip_count, dtype=jnp.int32)[None, :]
    ).astype(wide)
    first_mod = jnp.sum(onehot[:, :, None, None] * modulation[0][None], axis=1)
    second_mod = modulation[1]

    def layer_biases(layer):
        bias_query = tensor_part(proj_full[layer, 0])
        bias_value = tensor_part(proj_full[layer, 1])
        joined = jnp.concatenate([bias_query, jnp.zeros_like(bias_query), bias_value])
        return (
            jnp.pad(joined, (0, padded(joined_width) - joined_width))[None],
            proj_full[layer, 2:3],
            proj_full[layer, 3:4],
            lax.dynamic_slice_in_dim(hidden_full[layer], unit_start(units), units)[None],
        )

    def flat(values):
        return both_halves(values).reshape(-1, width)

    def own_places(values, frames):
        split = values.reshape(frames, 2, -1, width)
        return lax.dynamic_slice_in_dim(split, tensor, 1, 1)

    all_frames, own_place_count = frames_dev * dp_count, 2 * (place_half // dp_count)
    mods_0, mods_1 = first_mod, second_mod
    biases_0, biases_1 = layer_biases(0), layer_biases(1)

    upstream_1 = flat(out_grad)
    mlp_grad_1, turn_sums_1 = turn(upstream_1, mods_1)
    flat_grad_1 = pair_rows(*mlp_grad_1)

    wattn_0 = arrange(*after((*near_attn_0, *far_attn_0), own_attn_1))
    x_0 = flat(tokens)
    held = own_units_1
    hidden_0, joined_0, attended_0, both_0, middle_0, hidden_mlp = first_half(
        x_0, mods_0, wattn_0, biases_0, None, held
    )
    flat_0 = pair_rows(*hidden_mlp)
    units_0 = arrange(*after((*near_units_0, *far_units_0), near_attn_1, own_units_1))
    slope_0, active_0, keep, send = units_forward(
        after(flat_0, far_attn_1, flat_grad_1), units_0, biases_0[3]
    )
    branch_0 = pair_sum(chip_sum(keep, send))
    result_0 = own_places(block_result(middle_0, branch_0, biases_0, mods_0), frames_dev)
    arrived = lax.all_to_all(result_0, "dp", split_axis=2, concat_axis=0, tiled=True)
    x_1 = flat(after(arrived, near_units_1))

    wattn_1 = arrange(*near_attn_1, *far_attn_1)
    hidden_1, joined_1, attended_1, both_1, middle_1, hidden_mlp = first_half(
        x_1, mods_1, wattn_1, biases_1, own_place_count
    )
    flat_1 = pair_rows(*hidden_mlp)
    units_1 = arrange(*near_units_1, *far_units_1)
    slope_1, active_1, keep_1, send_1 = units_forward(flat_1, units_1, biases_1[3])

    inner_grad_1, keep, send, fc1_bias_1 = units_backward(flat_grad_1, units_1, slope_1)
    chip = chip_sum(keep, send)
    hidden_grad = pair_sum(chip)
    middle_grad, attn_grad_1, middle_sums_1 = middle_back(
        upstream_1, hidden_grad, middle_1, both_1, biases_1, mods_1
    )
    joined_grad_1, mine_grad, joined_bias_1 = attention_backward(
        attn_grad_1, wattn_1, joined_1, mods_1.shape[0], own_place_count
    )
    x_grad_1, input_sums_1 = input_back(middle_grad, mine_grad, x_1, mods_1, low)
    sent_back = own_places(x_grad_1, all_frames)
    arrived_back = lax.all_to_all(sent_back, "dp", split_axis=0, concat_axis=2, tiled=True)
    units_pairs = ((flat_1, inner_grad_1), (flat_grad_1, active_1))
    units_pairs = after(units_pairs, chip)
    start_units_1 = scatter_start(weight_grad(units_pairs))

    upstream_0 = flat(arrived_back)
    mlp_grad_0, turn_sums_0 = turn(upstream_0, mods_0)
    part_0 = mlp_grad_0[1]
    attn_pairs = (((hidden_1,), joined_grad_1), ((attn_grad_1,), attended_1))
    attn_pairs = after(attn_pairs, sent_back)
    start_attn_1 = scatter_start(weight_grad(attn_pairs))
    near_sums = scatter_near_sums(after(start_units_1, start_attn_1[0]))
    near_units_grad_1 = scatter_near(near_sums)
    flat_grad_0 = pair_rows(*mlp_grad_0)
    inner_grad_0, keep, send, fc1_bias_0 = units_backward(
        flat_grad_0, units_0, slope_0
    )
    chip = chip_sum(keep, send)
    hidden_grad = pair_sum(chip)
    middle_grad, attn_grad, middle_sums_0 = middle_back(
        upstream_0, hidden_grad, middle_0, both_0, biases_0, mods_0
    )
    blocks_units_1 = scatter_plane_blocks(near_units_grad_1)
    half_units_1 = scatter_halve(blocks_units_1)
    near_sums = scatter_near_sums(after(start_attn_1, chip))
    near_attn_grad_1 = scatter_near(near_sums)
    units_pairs = ((flat_0, inner_grad_0), (flat_grad_0, active_0))
    units_pairs = after(units_pairs, chip, blocks_units_1, near_sums)
    start_units_0 = scatter_start(weight_grad(units_pairs))
    blocks_attn_1 = scatter_plane_blocks(after(near_attn_grad_1, attn_grad))
    half_attn_1 = scatter_halve(blocks_attn_1)
    held = after(attn_grad, blocks_attn_1)
    joined_grad, mine_grad, joined_bias_0 = attention_backward(
        held, wattn_0, joined_0, mods_0.shape[0], None
    )
    attn_pairs = (((hidden_0,), joined_grad), ((attn_grad,), attended_0))
    parts = weight_grad(attn_pairs)
    held = after(parts, start_units_0, half_units_1, half_attn_1)
    start_attn_0 = scatter_start(held)
    near_sums = scatter_near_sums(after(start_units_0, parts[0]))
    near_units_grad_0 = scatter_near(near_sums)
    x_grad_0, input_sums_0 = input_back(
        after(middle_grad, parts[0]), mine_grad, x_0, mods_0, wide
    )
    tokens_grad = own_places(x_grad_0, frames_dev)
    gate_0 = gate_sums(upstream_0, branch_0, biases_0, mods_0)
    last_units_1 = scatter_last(after(half_units_1, parts[0]))
    blocks_units_0 = scatter_plane_blocks(after(near_units_grad_0, x_grad_0, last_units_1, gate_0))
    half_units_0 = scatter_halve(blocks_units_0)
    last_attn_1 = scatter_last(after(half_attn_1, x_grad_0))
    second_units = scatter_join(last_units_1, True)

    held = after((keep_1, send_1), attn_grad_1, sent_back)
    branch_1 = pair_sum(chip_sum(*held))
    output = own_places(block_result(middle_1, branch_1, biases_1, mods_1), all_frames)
    gate_1 = gate_sums(after(upstream_1, parts[0]), branch_1, biases_1, mods_1)

    input_sums_0 = after(input_sums_0, blocks_units_0, half_attn_1)
    packed_sums = pack_sums(
        clip_count,
        lax.axis_index("dp") * frames_dev,
        (
            (input_sums_0, middle_sums_0, gate_0, turn_sums_0, joined_bias_0, fc1_bias_0),
            (input_sums_1, middle_sums_1, gate_1, turn_sums_1, joined_bias_1, fc1_bias_1),
        ),
    )
    owned = jnp.sum(deal(packed_sums.reshape(all_devices, -1)), axis=0)
    near_sums = scatter_near_sums(after(start_attn_0, blocks_units_0, owned))
    near_attn_grad_0 = scatter_near(near_sums)
    held = after(owned, near_sums)
    everything = deal(jnp.broadcast_to(held[None], (all_devices, owned.shape[0])))
    held = after(near_attn_grad_0, everything, last_attn_1, half_units_0)
    sums_attn_0 = scatter_planes(scatter_plane_blocks(held))
    held = after(half_units_0, near_attn_grad_0, everything)
    first_units = scatter_join(scatter_last(held), True)
    second_attn = scatter_join(after(last_attn_1, near_attn_grad_0, everything))[0]
    first_attn = scatter_finish(sums_attn_0)
    everything = after(everything, sums_attn_0[0]).reshape(2, -1, width)
    mod_rows = 6 * clip_count
    summed_mod = everything[:, :mod_rows].reshape(2, clip_count, 6, width)
    b_ada_grad = lax.dynamic_slice_in_dim(jnp.sum(summed_mod, axis=1), own_start, own_width, 2)
    columns = everything[:, mod_rows + 2 : mod_rows + 6].reshape(2, 2, 2, width)[..., :head_width]
    proj_rows = jnp.concatenate(
        [
            jnp.concatenate([columns[:, 0], columns[:, 1]], axis=-1),
            everything[:, mod_rows : mod_rows + 2],
        ],
        axis=1,
    )
    b_proj_grad = lax.dynamic_slice_in_dim(proj_rows, own_start, own_width, 2)
    fc1_rows = everything[:, mod_rows + 6 :].reshape(2, -1)
    own_units = fc1_rows.shape[1] // all_devices
    b_fc1_grad = lax.dynamic_slice_in_dim(fc1_rows, flat_index * own_units, own_units, 1)
    w_ada_grad = sum(
        gated_own[clip][None, :, None, None] * summed_mod[:, clip][:, None]
        for clip in range(clip_count)
    )
    silu_grad = jnp.stack(
        [
            jnp.sum(summed_mod[:, clip][:, None] * w_ada_wide, axis=(0, 2, 3))
            for clip in range(clip_count)
        ]
    )
    cond_own = lax.dynamic_slice_in_dim(cond_float, own_start, own_width, 1)
    cond_grad = jax.vjp(jax.nn.silu, cond_own)[1](silu_grad)[0]

    reduced = ((first_attn, first_units), (second_attn, second_units))
    out_start = padded(joined_width)
    w_qkv_grad = jnp.stack(
        [part[0][:, :joined_width].reshape(own_rows, 3, head_width) for part in reduced]
    )
    w_out_grad = jnp.stack(
        [part[0][:, out_start : out_start + head_width].T for part in reduced]
    )
    w_fc1_grad = jnp.stack(
        [jnp.concatenate([part[1][0, :, :units], part[1][1, :, :units]], axis=1) for part in reduced]
    )
    w_fc2_grad = jnp.stack(
        [part[1][:, :, units:].transpose(0, 2, 1).reshape(2 * units, own_rows) for part in reduced]
    )
    return (
        output,
        tokens_grad,
        cond_grad,
        w_qkv_grad,
        w_out_grad,
        w_fc1_grad,
        w_fc2_grad,
        w_ada_grad,
        b_ada_grad,
        b_proj_grad,
        b_fc1_grad,
    )


def solution(mesh):
    return jax.shard_map(
        per_device,
        mesh=mesh,
        in_specs=(
            P("dp", "tensor", None, None),
            P(),
            P(None, "tensor", "dp", None),
            P(None, "dp", None, "tensor"),
            P(None, "tensor", "dp"),
            P(None, "dp", "tensor"),
            P(None, "tensor", "dp"),
            P(None, ("dp", "tensor"), None, None),
            P(None, None, ("dp", "tensor")),
            P(None, None, ("dp", "tensor")),
            P(None, ("dp", "tensor")),
        ),
        out_specs=(
            P(None, "tensor", "dp", None),
            P("dp", "tensor", None, None),
            P(None, ("dp", "tensor")),
            P(None, "dp", None, "tensor"),
            P(None, "tensor", "dp"),
            P(None, "dp", "tensor"),
            P(None, "tensor", "dp"),
            P(None, ("dp", "tensor"), None, None),
            P(None, None, ("dp", "tensor")),
            P(None, None, ("dp", "tensor")),
            P(None, ("dp", "tensor")),
        ),
        check_vma=False,
    )
```

```python
import functools

import jax
import jax.numpy as jnp
from jax import lax
from jax.experimental import pallas as pl
from jax.experimental.pallas import tpu as pltpu
from jax.sharding import PartitionSpec as P

HEAD_DIM = 72
FRAMES = 16


epsilon = 1e-06
highest = lax.Precision.HIGHEST
low = jnp.bfloat16
wide = jnp.float32
everyone = ("dp", "tensor")


def layer_norm(values):
    centred = values - jnp.mean(values, axis=-1, keepdims=True)
    inverse = lax.rsqrt(jnp.mean(centred * centred, axis=-1, keepdims=True) + epsilon)
    return (centred * inverse, inverse)


def layer_norm_back(normed, inverse, upstream):
    first_moment = jnp.mean(upstream, axis=-1, keepdims=True)
    second_moment = jnp.mean(upstream * normed, axis=-1, keepdims=True)
    return inverse * (upstream - first_moment - normed * second_moment)


def product(left_side, right_side):
    return jnp.dot(left_side, right_side, preferred_element_type=wide)


def product_left(left_side, right_side):
    return lax.dot_general(
        left_side, right_side, (((0,), (0,)), ((), ())), preferred_element_type=wide
    )


def product_right(left_side, right_side):
    return lax.dot_general(
        left_side, right_side, (((1,), (1,)), ((), ())), preferred_element_type=wide
    )


PAIR = 2


def swap_by(values, offset):
    count = lax.axis_size("dp")
    return lax.ppermute(values, "dp", [(i, i ^ offset) for i in range(count)])


def my_bit(bit):
    return (lax.axis_index("dp") >> bit) & 1


def after(values, *others):
    return lax.optimization_barrier((values,) + others)[0]


def pick(first, mine, theirs, axis):
    return jnp.stack(
        [jnp.where(first, mine, theirs), jnp.where(first, theirs, mine)], axis=axis
    )


def place_scalars():
    return jnp.stack(
        [lax.axis_index("tensor"), lax.axis_index("dp") & 3, lax.axis_index("dp") >> 2]
    ).astype(jnp.int32)


def gather_pair(shard):
    paired = isinstance(shard, tuple)
    own, sent = shard if paired else (shard, shard)
    return jnp.stack([own, swap_by(sent, 1 << PAIR)])


def gather_planes(held):
    while held.shape[0] * 4 < lax.axis_size("dp"):
        held = jnp.concatenate([held, swap_by(held, held.shape[0] * 4)])
    return held


def gather_straight(shard):
    paired = isinstance(shard, tuple)
    parts = [shard[0] if paired else shard]
    for relative in range(1, lax.axis_size("dp") // 4):
        sent = shard[relative & 1] if paired else shard
        parts.append(swap_by(sent, relative << 2))
    return jnp.stack(parts)


def arrange_kernel(place_ref, own_ref, across_ref, along_ref, low_ref, high_ref, out_ref):
    me = place_ref[1]
    out_ref[me] = own_ref[0]
    out_ref[me ^ 1] = across_ref[0]
    out_ref[me ^ 2] = along_ref[0]
    in_low = pl.program_id(0) < pl.num_programs(0) // 2

    @pl.when(in_low)
    def _():
        out_ref[me ^ 3] = low_ref[0]

    @pl.when(jnp.logical_not(in_low))
    def _():
        out_ref[me ^ 3] = high_ref[0]


def arrange(own, across, along, low_part, high_part):
    groups, rows, columns = own.shape
    half = groups // 2
    block = (1, rows, columns)
    whole = pl.BlockSpec(block, lambda i, place: (i, 0, 0))
    out = pl.pallas_call(
        arrange_kernel,
        out_shape=jax.ShapeDtypeStruct((groups * 4, rows, columns), own.dtype),
        grid_spec=pltpu.PrefetchScalarGridSpec(
            num_scalar_prefetch=1,
            grid=(groups,),
            in_specs=[
                whole,
                whole,
                whole,
                pl.BlockSpec(block, lambda i, place: (jnp.minimum(i, half - 1), 0, 0)),
                pl.BlockSpec(block, lambda i, place: (jnp.maximum(i - half, 0), 0, 0)),
            ],
            out_specs=pl.BlockSpec((4, rows, columns), lambda i, place: (i ^ place[2], 0, 0)),
        ),
        name="arrange",
        cost_estimate=cost(0, 16 * groups * rows * columns),
    )(place_scalars(), own, across, along, low_part, high_part)
    return out.reshape(groups * 4 * rows, columns)


def gather_near(own):
    return (own, swap_by(own, 1), swap_by(own, 2))


def gather_halves(near):
    half = near[0].shape[0] // 2
    return (near[1][:half], near[2][half:])


def gather_far(halves):
    return (swap_by(halves[0], 2), swap_by(halves[1], 1))


def weight_grad_kernel(count, starts, lefts, place_ref, *refs):
    pairs = len(starts)
    operands, outs = refs[: pairs * (lefts + 1)], refs[pairs * (lefts + 1) : -2]
    left_rows, total = refs[-2:]
    own, to_across, to_along, rest_across, rest_along = outs
    me, plane = place_ref[1], place_ref[2]
    rows, groups = total.shape[0] // count, count // 4
    half = groups // 2
    for index, start in enumerate(starts):
        *parts, right = operands[index * (lefts + 1) : (index + 1) * (lefts + 1)]
        if lefts == 1:
            left = parts[0][...]
        else:
            for at, part in enumerate(parts):
                left_rows[at * part.shape[0] : (at + 1) * part.shape[0]] = part[...]
            left = left_rows[...]
        total[:, start : start + right.shape[1]] = product_left(left, right[...])
        spare = -right.shape[1] % 128
        if spare:
            end = start + right.shape[1]
            total[:, end : end + spare] = jnp.zeros((total.shape[0], spare), wide)

    def copy(out, at, mate, first, length):
        place = me ^ mate
        if rows % 8 == 0:

            @pl.loop(0, length)
            def _(step):
                chip = (plane ^ (first + step)) * 4 + place
                out[at + step] = total[pl.ds(pl.multiple_of(chip * rows, 8), rows), :].astype(low)

        else:

            for chip in range(count):

                @pl.when((chip & 3) == place)
                def _(chip=chip):
                    step = (plane ^ (chip >> 2)) - first

                    @pl.when((step >= 0) & (step < length))
                    def _():
                        out[at + step] = total[chip * rows : (chip + 1) * rows, :].astype(low)

    copy(to_along, 0, 3, 0, half)
    copy(to_along, half, 2, 0, half)
    copy(to_across, 0, 3, half, half)
    copy(to_across, half, 1, half, half)
    copy(rest_across, 0, 1, 0, half)
    copy(rest_along, 0, 2, half, half)
    copy(own, 0, 0, 0, groups)


def weight_grad(pairs):
    count = lax.axis_size("dp")
    groups = count // 4
    half = groups // 2
    lefts = len(pairs[0][0])
    width = pairs[0][0][0].shape[1]
    rows = width // count
    starts, columns = [], 0
    for _, right in pairs:
        starts.append(columns)
        columns += padded(right.shape[1])
    tokens = pairs[0][1].shape[0]
    own, to_across, to_along, rest_across, rest_along = pl.pallas_call(
        functools.partial(weight_grad_kernel, count, tuple(starts), lefts),
        out_shape=[
            jax.ShapeDtypeStruct((blocks, rows, columns), low)
            for blocks in (groups, groups, groups, half, half)
        ],
        in_specs=[pl.BlockSpec(memory_space=pltpu.SMEM)]
        + [pl.BlockSpec(memory_space=pltpu.VMEM)] * ((lefts + 1) * len(pairs)),
        scratch_shapes=[pltpu.VMEM((tokens, width), low), pltpu.VMEM((width, columns), wide)],
        name="weight_grad",
        cost_estimate=cost(
            2 * tokens * width * columns, 2 * width * columns + 4 * tokens * (width + columns)
        ),
    )(place_scalars(), *[operand for left, right in pairs for operand in (*left, right)])
    return (own, rest_across, rest_along, to_across, to_along)


def scatter_start(parts):
    own, rest_across, rest_along, to_across, to_along = parts
    return (own, rest_across, rest_along, swap_by(to_across, 1), swap_by(to_along, 2))


def scatter_near_sums(state):
    own, rest_across, rest_along, got_across, got_along = state
    half = rest_across.shape[0]
    rest_across = (rest_across.astype(wide) + got_along[:half].astype(wide)).astype(low)
    rest_along = (rest_along.astype(wide) + got_across[:half].astype(wide)).astype(low)
    return (own, got_across, got_along, rest_across, rest_along)


def scatter_near(sums):
    own, got_across, got_along, rest_across, rest_along = sums
    return (own, got_across, got_along, swap_by(rest_across, 1), swap_by(rest_along, 2))


def scatter_plane_blocks(state):
    own, got_across, got_along, last_across, last_along = state
    half = own.shape[0] // 2

    def total(relative):
        block = own[relative].astype(wide)
        if relative < half:
            return block + got_along[half + relative].astype(wide) + last_across[relative].astype(wide)
        return block + got_across[relative].astype(wide) + last_along[relative - half].astype(wide)

    return [total(relative) for relative in range(own.shape[0])]


def scatter_planes(blocks):
    got = [
        swap_by(block.astype(low), relative << 2) for relative, block in enumerate(blocks) if relative
    ]
    return (blocks[0], got)


def scatter_finish(state, paired=False):
    own, got = state
    got = [part.astype(wide) for part in got]
    if paired:
        return pick(my_bit(PAIR) == 0, own + sum(got[1::2]), sum(got[0::2]), 0)
    return own + sum(got)


def scatter_halve(blocks):
    half = len(blocks) // 2
    sent = jnp.stack([block.astype(low) for block in blocks[half:]])
    return (blocks[:half], swap_by(sent, half * 4))


def scatter_join(state, paired=False):
    kept, got = state
    if paired:
        return pick(my_bit(PAIR) == 0, kept[0], got[0].astype(wide), 0)
    return [block + got[index].astype(wide) for index, block in enumerate(kept)]


def scatter_last(state):
    blocks = scatter_join(state)
    while len(blocks) > 2:
        blocks = scatter_join(scatter_halve(blocks))
    return scatter_halve(blocks)


def swap_tensor(values):
    return lax.ppermute(values, "tensor", [(0, 1), (1, 0)])


def both_halves(values):
    return lax.all_gather(values, "tensor", axis=1, tiled=True)


def own_half(values):
    return lax.dynamic_slice_in_dim(
        values, lax.axis_index("tensor") * (values.shape[1] // 2), values.shape[1] // 2, 1
    )


def pair_part(values):
    half = values.shape[0] // 2
    return lax.dynamic_slice_in_dim(values, lax.axis_index("tensor") * half, half, 0)


def pair_rows(values, sent):
    got = swap_by(sent, 1 << PAIR)
    return (values, lax.all_gather(got, "tensor", axis=0, tiled=True))


def chip_sum(keep, send):
    return keep.astype(wide) + swap_tensor(send).astype(wide)


def pair_sum(chip):
    got = swap_by(chip[1].astype(low), 1 << PAIR)
    total = (chip[0] + got.astype(wide)).astype(low)
    return lax.all_gather(total, "tensor", axis=0, tiled=True)


def unit_start(units):
    return (lax.axis_index("tensor") * 2 + my_bit(PAIR)) * units


def deal(values):
    return lax.all_to_all(values, everyone, split_axis=0, concat_axis=0, tiled=True)


def sum_to_owner(values, owners):
    lead = values.shape[:-1]
    dealt = jnp.moveaxis(values.reshape(lead + (owners, -1)), -2, 0)
    return dealt.reshape(owners, -1)


def from_owners(values, lead):
    owners = values.shape[0]
    return jnp.moveaxis(values.reshape((owners,) + lead + (-1,)), 0, -2).reshape(lead + (-1,))


def padded(width):
    return width + -width % 128


def fixed(*shape):
    return pl.BlockSpec(shape, lambda i, *_: (0,) * len(shape))


def by_rows(rows, *rest):
    return pl.BlockSpec((rows,) + rest, lambda i, *_: (i,) + (0,) * len(rest))


COST_SHARE = 16


def by_group(*rest):
    return pl.BlockSpec((1,) + rest, lambda i, *_: (i // STEPS,) + (0,) * len(rest))


def cost(flops, bytes_accessed, transcendentals=0):
    return pl.CostEstimate(
        flops=flops // COST_SHARE,
        bytes_accessed=bytes_accessed // COST_SHARE,
        transcendentals=transcendentals // COST_SHARE,
    )


STEPS = 2


def add_sums(sums_ref, *values):
    @pl.when(lax.rem(pl.program_id(0), STEPS) == 0)
    def _():
        sums_ref[...] = jnp.zeros_like(sums_ref)

    for row, value in enumerate(values):
        sums_ref[0, row : row + 1] += column_sum(value)


def column_sum(values):
    return jnp.sum(values, axis=0, keepdims=True)


def same_place(rows, place_count):
    if rows == place_count:
        return None
    first = lax.broadcasted_iota(jnp.int32, (rows, rows), 0)
    second = lax.broadcasted_iota(jnp.int32, (rows, rows), 1)
    return lax.rem(first, place_count) == lax.rem(second, place_count)


def head_probs(query, keys, mask):
    scores = product_right(query, keys) * (HEAD_DIM ** (-0.5))
    if mask is not None:
        scores = jnp.where(mask, scores, -1e30)
    exponent = jnp.exp(scores - jnp.max(scores, axis=-1, keepdims=True))
    return exponent * (1.0 / jnp.sum(exponent, axis=-1, keepdims=True))


def attention_kernel(
    place_count, x_ref, mod_ref, weight_ref, bias_ref, hidden_ref, joined_ref, attended_ref, out_ref
):
    rows, width = attended_ref.shape
    joined_width = joined_ref.shape[1]
    normed, _ = layer_norm(x_ref[...].astype(wide))
    hidden = (normed * (1.0 + mod_ref[0, 1:2]) + mod_ref[0, 0:1]).astype(low)
    hidden_ref[...] = hidden
    joined_ref[...] = (product(hidden, weight_ref[:, :joined_width]) + bias_ref[...]).astype(low)
    mask = None if place_count is None else same_place(rows, place_count)
    for start in range(0, width, HEAD_DIM):
        query, keys, value = (
            joined_ref[:, part * width + start : part * width + start + HEAD_DIM]
            for part in range(3)
        )
        probs = head_probs(query, keys, mask).astype(low)
        attended_ref[:, start : start + HEAD_DIM] = product(probs, value).astype(low)
    out_ref[...] = product_right(
        attended_ref[...], weight_ref[:, joined_width : joined_width + width]
    ).astype(low)


def attention_back_kernel(
    place_count, upstream_ref, weight_ref, joined_ref, grad_ref, out_ref, bias_ref
):
    rows, joined_width = joined_ref.shape
    width = upstream_ref.shape[1] // 2
    score_scale = HEAD_DIM ** (-0.5)
    attended_grad = product(
        upstream_ref[...], weight_ref[:, joined_width : joined_width + width]
    ).astype(low)
    mask = None if place_count is None else same_place(rows, place_count)
    for start in range(0, width, HEAD_DIM):
        query, keys, value = (
            joined_ref[:, part * width + start : part * width + start + HEAD_DIM]
            for part in range(3)
        )
        upstream = attended_grad[:, start : start + HEAD_DIM]
        scores = product_right(keys, query) * score_scale
        if mask is not None:
            scores = jnp.where(mask, scores, -1e30)
        exponent = jnp.exp(scores - jnp.max(scores, axis=0, keepdims=True))
        probs = exponent * (1.0 / jnp.sum(exponent, axis=0, keepdims=True))
        value_grad = product(probs.astype(low), upstream)
        prob_grad = product_right(value, upstream)
        centre = jnp.sum(probs * prob_grad, axis=0, keepdims=True)
        score_grad = (probs * (prob_grad - centre)).astype(low)
        query_grad = product_left(score_grad, keys) * score_scale
        keys_grad = product(score_grad, query) * score_scale
        for part, grad in enumerate((query_grad, keys_grad, value_grad)):
            grad_ref[:, part * width + start : part * width + start + HEAD_DIM] = grad.astype(low)
    spare = joined_width - 3 * width
    if spare:
        grad_ref[:, 3 * width :] = jnp.zeros((rows, spare), low)
    joined_grad = grad_ref[...]
    bias_ref[0] = column_sum(joined_grad.astype(wide))
    out_ref[...] = product_right(joined_grad, weight_ref[:, :joined_width]).astype(low)


def middle_kernel(x_ref, mine_ref, theirs_ref, bias_ref, mod_ref, middle_ref, hidden_ref):
    branch = mine_ref[...].astype(wide) + theirs_ref[...].astype(wide) + bias_ref[...]
    middle = x_ref[...].astype(wide) + mod_ref[0, 2:3] * branch
    middle_ref[...] = middle
    normed, _ = layer_norm(middle)
    hidden_ref[...] = (normed * (1.0 + mod_ref[0, 4:5]) + mod_ref[0, 3:4]).astype(low)


def split_halves(place_ref, partial_ref, keep_ref, send_ref):
    tensor = place_ref[0]
    half = keep_ref.shape[1]
    keep_ref[0] = partial_ref[pl.ds(pl.multiple_of(tensor * half, 8), half), :].astype(low)
    send_ref[0] = partial_ref[pl.ds(pl.multiple_of((1 - tensor) * half, 8), half), :].astype(low)


def gelu_parts(values):
    root = 0.7978845608028654
    square = values * values
    bend = jnp.tanh(root * (values + 0.044715 * values * square))
    share = 0.5 * (1.0 + bend)
    steep = 0.5 * root * (1.0 - bend * bend) * (1.0 + 3.0 * 0.044715 * square)
    return (values * share, share + values * steep)


def units_kernel(
    place_ref,
    own_ref,
    other_ref,
    up_ref,
    down_ref,
    bias_ref,
    slope_ref,
    active_ref,
    keep_ref,
    send_ref,
    partial_ref,
):
    hidden = jnp.where(pl.program_id(0) == 0, own_ref[...], other_ref[...])
    inner = product(hidden, up_ref[...]) + bias_ref[...]
    active, slope = gelu_parts(inner)
    slope_ref[...] = slope.astype(low)
    active = active.astype(low)
    active_ref[...] = active
    partial_ref[...] = product_right(active, down_ref[...])
    split_halves(place_ref, partial_ref, keep_ref, send_ref)


def units_back_kernel(
    place_ref,
    own_ref,
    other_ref,
    up_ref,
    down_ref,
    slope_ref,
    grad_ref,
    keep_ref,
    send_ref,
    bias_ref,
    partial_ref,
):
    upstream = jnp.where(pl.program_id(0) == 0, own_ref[...], other_ref[...])
    grad = (product(upstream, down_ref[...]) * slope_ref[...].astype(wide)).astype(low)
    grad_ref[...] = grad

    @pl.when(pl.program_id(0) == 0)
    def _():
        bias_ref[...] = jnp.zeros_like(bias_ref)

    bias_ref[...] += column_sum(grad.astype(wide))
    partial_ref[...] = product_right(grad, up_ref[...])
    split_halves(place_ref, partial_ref, keep_ref, send_ref)


def result_kernel(middle_ref, branch_ref, bias_ref, mod_ref, out_ref):
    branch = branch_ref[...].astype(wide) + bias_ref[...]
    out_ref[...] = (middle_ref[...] + mod_ref[0, 5:6] * branch).astype(low)


def turn_kernel(upstream_ref, mod_ref, grad_ref, sums_ref):
    grad = (upstream_ref[...].astype(wide) * mod_ref[0, 5:6]).astype(low)
    grad_ref[...] = grad
    add_sums(sums_ref, grad.astype(wide))


def gate_kernel(upstream_ref, branch_ref, bias_ref, mod_ref, sums_ref):
    branch = branch_ref[...].astype(wide) + bias_ref[...]
    add_sums(sums_ref, upstream_ref[...].astype(wide) * branch)


def middle_back_kernel(
    upstream_ref,
    hidden_ref,
    middle_ref,
    mine_ref,
    theirs_ref,
    bias_ref,
    mod_ref,
    out_ref,
    grad_ref,
    sums_ref,
):
    normed, inverse = layer_norm(middle_ref[...])
    hidden_grad = hidden_ref[...].astype(wide)
    middle_grad = upstream_ref[...].astype(wide) + layer_norm_back(
        normed, inverse, hidden_grad * (1.0 + mod_ref[0, 4:5])
    )
    out_ref[...] = middle_grad
    grad = (middle_grad * mod_ref[0, 2:3]).astype(low)
    grad_ref[...] = grad
    branch = mine_ref[...].astype(wide) + theirs_ref[...].astype(wide) + bias_ref[...]
    add_sums(
        sums_ref, hidden_grad, hidden_grad * normed, middle_grad * branch, grad.astype(wide)
    )


def input_back_kernel(middle_ref, mine_ref, theirs_ref, x_ref, mod_ref, out_ref, sums_ref):
    normed, inverse = layer_norm(x_ref[...].astype(wide))
    hidden_grad = mine_ref[...].astype(wide) + theirs_ref[...].astype(wide)
    out_ref[...] = (
        middle_ref[...] + layer_norm_back(normed, inverse, hidden_grad * (1.0 + mod_ref[0, 1:2]))
    ).astype(out_ref.dtype)
    add_sums(sums_ref, hidden_grad, hidden_grad * normed)


def array(dtype, *shape):
    return jax.ShapeDtypeStruct(shape, dtype)


def attention_forward(x, mods, weight, bias, place_count):
    rows, width = x.shape
    groups = mods.shape[0]
    block = rows // groups
    part, joined = width // 2, bias.shape[1]
    return pl.pallas_call(
        functools.partial(attention_kernel, place_count),
        grid=(groups,),
        in_specs=[
            by_rows(block, width),
            by_rows(1, 6, width),
            fixed(*weight.shape),
            fixed(*bias.shape),
        ],
        out_specs=[by_rows(block, n) for n in (width, joined, part, width)],
        out_shape=[array(low, rows, n) for n in (width, joined, part, width)],
        name="attention",
        cost_estimate=cost(
            2 * rows * width * (joined + part) + 4 * rows * block * part,
            2 * weight.size + 2 * rows * (3 * width + joined + part),
            rows * block * part // HEAD_DIM,
        ),
    )(x, mods, weight, bias)


def attention_backward(upstream, weight, joined, groups, place_count):
    rows, width = upstream.shape
    block = rows // groups
    columns = joined.shape[1]
    return pl.pallas_call(
        functools.partial(attention_back_kernel, place_count),
        grid=(groups,),
        in_specs=[by_rows(block, width), fixed(*weight.shape), by_rows(block, columns)],
        out_specs=[by_rows(block, columns), by_rows(block, width), by_rows(1, 1, columns)],
        out_shape=[
            array(low, rows, columns),
            array(low, rows, width),
            array(wide, groups, 1, columns),
        ],
        name="attention_back",
        cost_estimate=cost(
            2 * rows * width * weight.shape[1] + 5 * rows * block * width,
            2 * weight.size + 2 * rows * (2 * width + 2 * columns),
            rows * block * width // (2 * HEAD_DIM),
        ),
    )(upstream, weight, joined)


def row_kernel(body, groups, row_inputs, fixed_inputs, mods, outs, sums, name, sent=None):
    rows, width = row_inputs[0].shape
    block = rows // (groups * STEPS)
    sum_shape = [array(wide, groups, 8, width)] * sums
    moved = sum(item.size * item.dtype.itemsize for item in row_inputs)
    first_out = len(row_inputs) + len(fixed_inputs) + 1
    alone = sent is not None and groups == 1 and STEPS == 2

    def steps(place_ref, *refs):
        body(*refs[:-1])

        @pl.when(pl.program_id(0) == place_ref[0])
        def _():
            refs[-1][...] = refs[first_out + sent][...]

    results = pl.pallas_call(
        steps if alone else body,
        grid_spec=pltpu.PrefetchScalarGridSpec(
            num_scalar_prefetch=int(alone),
            grid=(groups * STEPS,),
            in_specs=[by_rows(block, width) for _ in row_inputs]
            + [fixed(*item.shape) for item in fixed_inputs]
            + [by_group(6, width)],
            out_specs=[by_rows(block, width) for _ in outs]
            + [by_group(8, width)] * sums
            + [fixed(block, width)] * alone,
        ),
        out_shape=[array(dtype, rows, width) for dtype in outs]
        + sum_shape
        + [array(low, block, width)] * alone,
        name=name,
        cost_estimate=cost(20 * rows * width, moved + 4 * rows * width * len(outs)),
    )(*[place_scalars()] * alone, *row_inputs, *fixed_inputs, mods)
    if sent is not None and not alone:
        results = [*results, pair_part(results[sent])]
    return results


def units_call(body, rows_in, updown, extra, extra_spec, outs, out_specs, name):
    half, width = rows_in[0].shape
    units = updown.shape[1] // 2
    rows = 2 * half
    halves = array(low, 2, half // 2, width)
    at = pl.BlockSpec((1, half // 2, width), lambda i, *_: (i, 0, 0))
    return pl.pallas_call(
        body,
        grid_spec=pltpu.PrefetchScalarGridSpec(
            num_scalar_prefetch=1,
            grid=(2,),
            in_specs=[
                fixed(half, width),
                fixed(half, width),
                pl.BlockSpec((width, units), lambda i, *_: (0, 0)),
                pl.BlockSpec((width, units), lambda i, *_: (0, 1)),
                extra_spec,
            ],
            out_specs=out_specs[: len(outs) - 1] + [at, at] + out_specs[len(outs) - 1 :]
            if name == "units_back"
            else out_specs + [at, at],
            scratch_shapes=[pltpu.VMEM((half, width), wide)],
        ),
        out_shape=outs[:-1] + [halves, halves] + outs[-1:]
        if name == "units_back"
        else outs + [halves, halves],
        name=name,
        cost_estimate=cost(
            4 * rows * width * units,
            4 * width * units + 4 * rows * width + 6 * rows * units,
            rows * units,
        ),
    )(place_scalars(), *rows_in, updown, updown, extra)


def units_forward(hidden, updown, bias):
    rows, units = 2 * hidden[0].shape[0], updown.shape[1] // 2
    block = by_rows(rows // 2, units)
    return units_call(
        units_kernel,
        hidden,
        updown,
        bias,
        fixed(1, units),
        [array(low, rows, units), array(low, rows, units)],
        [block, block],
        "units",
    )


def units_backward(upstream, updown, slope):
    rows, units = slope.shape
    block = by_rows(rows // 2, units)
    return units_call(
        units_back_kernel,
        upstream,
        updown,
        slope,
        block,
        [array(low, rows, units), array(wide, 1, units)],
        [block, fixed(1, units)],
        "units_back",
    )


def first_half(x, mods, wattn, biases, place_count, *others):
    hidden, joined, attended, mine = attention_forward(x, mods, wattn, biases[0], place_count)
    both = after((mine, swap_tensor(mine)), *others)
    middle, hidden_mlp, sent = row_kernel(
        middle_kernel, mods.shape[0], (x, *both), (biases[1],), mods, (wide, low), 0, "middle", 1
    )
    return (hidden, joined, attended, both, middle, (hidden_mlp, sent))


def block_result(middle, branch, biases, mods):
    return row_kernel(
        result_kernel, mods.shape[0], (middle, branch), (biases[2],), mods, (low,), 0, "result"
    )[0]


def turn(upstream, mods):
    grad, sums, sent = row_kernel(
        turn_kernel, mods.shape[0], (upstream,), (), mods, (low,), 1, "turn", 0
    )
    return (grad, sent), sums


def gate_sums(upstream, branch, biases, mods):
    return row_kernel(
        gate_kernel, mods.shape[0], (upstream, branch), (biases[2],), mods, (), 1, "gate"
    )[0]


def middle_back(upstream, hidden_grad, middle, both, biases, mods):
    return row_kernel(
        middle_back_kernel,
        mods.shape[0],
        (upstream, hidden_grad, middle, *both),
        (biases[1],),
        mods,
        (wide, low),
        1,
        "middle_back",
    )


def input_back(middle_grad, mine_grad, x, mods, grad_dtype):
    return row_kernel(
        input_back_kernel,
        mods.shape[0],
        (middle_grad, mine_grad, swap_tensor(mine_grad), x),
        (),
        mods,
        (grad_dtype,),
        1,
        "input_back",
    )


def pack_kernel(clips, scalars_ref, *refs):
    out = refs[-1]
    tensor, pair, first_frame = scalars_ref[0], scalars_ref[1], scalars_ref[2]
    out[...] = jnp.zeros_like(out)
    per_block = out.shape[0] // 2
    width = out.shape[1]
    for block in range(2):
        inputs, middles, gate, turned, joined, fc1 = refs[6 * block : 6 * block + 6]
        base = block * per_block
        for group in range(gate.shape[0]):
            clip = group if block else lax.div(first_frame + group, FRAMES)
            if clips == 1:
                clip = 0
            parts = (
                (inputs, 0), (inputs, 1), (middles, 2), (middles, 0), (middles, 1), (gate, 0)
            )
            for index, (ref, row) in enumerate(parts):
                out[pl.ds(base + clip * 6 + index, 1), :] += 0.5 * ref[group, row : row + 1]
            place = base + clips * 6
            out[place : place + 1, :] += 0.5 * middles[group, 3:4]
            out[place + 1 : place + 2, :] += 0.5 * turned[group, 0:1]
            at = place + 2 + 2 * tensor
            spare = joined.shape[2] - width
            out[pl.ds(at, 1), :] += joined[group, :, :width]
            out[pl.ds(at + 1, 1), :spare] += joined[group, :, width:]
        out[pl.ds(base + clips * 6 + 6 + 2 * tensor + pair, 1), :] += fc1[...]


def pack_sums(clips, first_frame, blocks):
    width = blocks[0][0].shape[2]
    rows = 2 * (6 * clips + 10)
    scalars = jnp.stack([lax.axis_index("tensor"), my_bit(PAIR), first_frame]).astype(jnp.int32)
    operands = [item for block in blocks for item in block]
    return pl.pallas_call(
        functools.partial(pack_kernel, clips),
        out_shape=array(wide, rows, width),
        in_specs=[pl.BlockSpec(memory_space=pltpu.SMEM)]
        + [pl.BlockSpec(memory_space=pltpu.VMEM)] * len(operands),
        name="pack",
        cost_estimate=cost(rows * width, 8 * rows * width),
    )(scalars, *operands)


def tensor_part(values):
    part = values.shape[-1] // 2
    return lax.dynamic_slice_in_dim(
        values, lax.axis_index("tensor") * part, part, values.ndim - 1
    )


def per_device(tokens, cond, out_grad, w_qkv, w_out, w_fc1, w_fc2, w_ada, b_ada, b_proj, b_fc1):
    dp_count = lax.axis_size("dp")
    all_devices = lax.axis_size(everyone)
    flat_index = lax.axis_index(everyone)
    tensor = lax.axis_index("tensor")
    width = tokens.shape[3]
    clip_count = cond.shape[0]
    own_rows, head_width = w_qkv.shape[1], w_qkv.shape[3]
    units = w_fc1.shape[2] // 2
    own_width = width // all_devices
    own_start = flat_index * own_width
    joined_width = 3 * head_width

    def pad_columns(values):
        return jnp.pad(values, ((0, 0), (0, padded(values.shape[1]) - values.shape[1])))

    def units_part(layer, side):
        first = side * units
        return jnp.concatenate(
            [
                lax.dynamic_slice_in_dim(w_fc1[layer], first, units, 1),
                lax.dynamic_slice_in_dim(w_fc2[layer], first, units, 0).T,
            ],
            axis=1,
        )

    shards = []
    for layer in range(2):
        shards.append(
            jnp.concatenate(
                [
                    pad_columns(w_qkv[layer].reshape(own_rows, joined_width)),
                    pad_columns(w_out[layer].T),
                ],
                axis=1,
            )
        )
        shards.append((units_part(layer, my_bit(PAIR)), units_part(layer, 1 - my_bit(PAIR))))
    cond_float = cond.astype(wide)
    gated_low = jax.nn.silu(cond_float).astype(low)
    gated_own = lax.dynamic_slice_in_dim(gated_low, own_start, own_width, 1).astype(wide)
    w_ada_wide = w_ada.astype(wide)
    partial_mod = jnp.stack(
        [
            jnp.sum(gated_own[clip][None, :, None, None] * w_ada_wide, axis=1)
            for clip in range(clip_count)
        ],
        axis=1,
    )
    own_mod = jnp.sum(deal(sum_to_owner(partial_mod, all_devices)), axis=0).reshape(
        2, clip_count, 6, own_width
    )
    own_mod = own_mod + b_ada.astype(wide)[:, None]
    pieces = (own_mod, b_proj.astype(wide), b_fc1.astype(wide))
    packed = jnp.concatenate([piece.reshape(-1) for piece in pieces])
    dealt = deal(jnp.broadcast_to(packed[None], (all_devices, packed.shape[0])))

    own_attn_0 = gather_straight(shards[0])
    near_attn_0 = gather_near(after(own_attn_0, dealt))
    own_units_0 = gather_straight(after(shards[1], own_attn_0))
    pair_attn_1 = gather_pair(after(shards[2], own_attn_0, own_units_0, near_attn_0))
    pair_units_1 = gather_pair(after(shards[3], pair_attn_1, near_attn_0))
    far_attn_0 = gather_far(gather_halves(near_attn_0))
    near_units_0 = gather_near(own_units_0)
    own_attn_1 = gather_planes(pair_attn_1)
    own_units_1 = gather_planes(after(pair_units_1, own_attn_1))
    near_attn_1 = gather_near(after(own_attn_1, near_attn_0, far_attn_0))
    far_units_0 = gather_far(gather_halves(near_units_0))
    near_units_1 = gather_near(after(own_units_1, near_units_0))
    far_attn_1 = gather_far(gather_halves(near_attn_1))
    far_units_1 = gather_far(gather_halves(near_units_1))
    dealt = after(dealt, near_units_0)
    first_end, second_end = pieces[0].size, pieces[0].size + pieces[1].size
    modulation = from_owners(dealt[:, :first_end], (2, clip_count, 6))
    proj_full = from_owners(dealt[:, first_end:second_end], (2, 4))
    hidden_full = from_owners(dealt[:, second_end:], (2,))

    frames_dev, place_half = tokens.shape[0], tokens.shape[2]
    frame_ids = lax.axis_index("dp") * frames_dev + jnp.arange(frames_dev, dtype=jnp.int32)
    onehot = (
        frame_ids[:, None] // FRAMES == jnp.arange(clip_count, dtype=jnp.int32)[None, :]
    ).astype(wide)
    first_mod = jnp.sum(onehot[:, :, None, None] * modulation[0][None], axis=1)
    second_mod = modulation[1]

    def layer_biases(layer):
        bias_query = tensor_part(proj_full[layer, 0])
        bias_value = tensor_part(proj_full[layer, 1])
        joined = jnp.concatenate([bias_query, jnp.zeros_like(bias_query), bias_value])
        return (
            jnp.pad(joined, (0, padded(joined_width) - joined_width))[None],
            proj_full[layer, 2:3],
            proj_full[layer, 3:4],
            lax.dynamic_slice_in_dim(hidden_full[layer], unit_start(units), units)[None],
        )

    def flat(values):
        return both_halves(values).reshape(-1, width)

    def own_places(values, frames):
        split = values.reshape(frames, 2, -1, width)
        return lax.dynamic_slice_in_dim(split, tensor, 1, 1)

    all_frames, own_place_count = frames_dev * dp_count, 2 * (place_half // dp_count)
    mods_0, mods_1 = first_mod, second_mod
    biases_0, biases_1 = layer_biases(0), layer_biases(1)

    upstream_1 = flat(out_grad)
    mlp_grad_1, turn_sums_1 = turn(upstream_1, mods_1)
    flat_grad_1 = pair_rows(*mlp_grad_1)

    wattn_0 = arrange(*after((*near_attn_0, *far_attn_0), own_attn_1))
    x_0 = flat(tokens)
    held = own_units_1
    hidden_0, joined_0, attended_0, both_0, middle_0, hidden_mlp = first_half(
        x_0, mods_0, wattn_0, biases_0, None, held
    )
    flat_0 = pair_rows(*hidden_mlp)
    units_0 = arrange(*after((*near_units_0, *far_units_0), near_attn_1, own_units_1))
    slope_0, active_0, keep, send = units_forward(
        after(flat_0, far_attn_1, flat_grad_1), units_0, biases_0[3]
    )
    branch_0 = pair_sum(chip_sum(keep, send))
    result_0 = own_places(block_result(middle_0, branch_0, biases_0, mods_0), frames_dev)
    arrived = lax.all_to_all(result_0, "dp", split_axis=2, concat_axis=0, tiled=True)
    x_1 = flat(after(arrived, near_units_1))

    wattn_1 = arrange(*near_attn_1, *far_attn_1)
    hidden_1, joined_1, attended_1, both_1, middle_1, hidden_mlp = first_half(
        x_1, mods_1, wattn_1, biases_1, own_place_count
    )
    flat_1 = pair_rows(*hidden_mlp)
    units_1 = arrange(*near_units_1, *far_units_1)
    slope_1, active_1, keep_1, send_1 = units_forward(flat_1, units_1, biases_1[3])

    inner_grad_1, keep, send, fc1_bias_1 = units_backward(flat_grad_1, units_1, slope_1)
    chip = chip_sum(keep, send)
    hidden_grad = pair_sum(chip)
    middle_grad, attn_grad_1, middle_sums_1 = middle_back(
        upstream_1, hidden_grad, middle_1, both_1, biases_1, mods_1
    )
    joined_grad_1, mine_grad, joined_bias_1 = attention_backward(
        attn_grad_1, wattn_1, joined_1, mods_1.shape[0], own_place_count
    )
    x_grad_1, input_sums_1 = input_back(middle_grad, mine_grad, x_1, mods_1, low)
    sent_back = own_places(x_grad_1, all_frames)
    arrived_back = lax.all_to_all(sent_back, "dp", split_axis=0, concat_axis=2, tiled=True)
    units_pairs = ((flat_1, inner_grad_1), (flat_grad_1, active_1))
    units_pairs = after(units_pairs, chip)
    start_units_1 = scatter_start(weight_grad(units_pairs))

    upstream_0 = flat(arrived_back)
    mlp_grad_0, turn_sums_0 = turn(upstream_0, mods_0)
    part_0 = mlp_grad_0[1]
    attn_pairs = (((hidden_1,), joined_grad_1), ((attn_grad_1,), attended_1))
    attn_pairs = after(attn_pairs, sent_back)
    start_attn_1 = scatter_start(weight_grad(attn_pairs))
    near_sums = scatter_near_sums(after(start_units_1, start_attn_1[0]))
    near_units_grad_1 = scatter_near(near_sums)
    flat_grad_0 = pair_rows(*mlp_grad_0)
    inner_grad_0, keep, send, fc1_bias_0 = units_backward(
        flat_grad_0, units_0, slope_0
    )
    chip = chip_sum(keep, send)
    hidden_grad = pair_sum(chip)
    middle_grad, attn_grad, middle_sums_0 = middle_back(
        upstream_0, hidden_grad, middle_0, both_0, biases_0, mods_0
    )
    blocks_units_1 = scatter_plane_blocks(after(near_units_grad_1, attn_grad))
    half_units_1 = scatter_halve(blocks_units_1)
    near_sums = scatter_near_sums(after(start_attn_1, chip))
    near_attn_grad_1 = scatter_near(near_sums)
    units_pairs = ((flat_0, inner_grad_0), (flat_grad_0, active_0))
    units_pairs = after(units_pairs, chip, blocks_units_1, near_sums)
    start_units_0 = scatter_start(weight_grad(units_pairs))
    blocks_attn_1 = scatter_plane_blocks(after(near_attn_grad_1, attn_grad))
    half_attn_1 = scatter_halve(blocks_attn_1)
    held = after(attn_grad, blocks_attn_1, start_units_0[0])
    joined_grad, mine_grad, joined_bias_0 = attention_backward(
        held, wattn_0, joined_0, mods_0.shape[0], None
    )
    attn_pairs = (((hidden_0,), joined_grad), ((attn_grad,), attended_0))
    parts = weight_grad(attn_pairs)
    held = after(parts, start_units_0, half_units_1, half_attn_1)
    start_attn_0 = scatter_start(held)
    near_sums = scatter_near_sums(start_units_0)
    near_units_grad_0 = scatter_near(near_sums)
    x_grad_0, input_sums_0 = input_back(
        after(middle_grad, parts[0], near_sums), mine_grad, x_0, mods_0, wide
    )
    tokens_grad = own_places(x_grad_0, frames_dev)
    gate_0 = gate_sums(after(upstream_0, parts[0]), branch_0, biases_0, mods_0)
    last_units_1 = scatter_last(after(half_units_1, parts[0]))
    blocks_units_0 = scatter_plane_blocks(after(near_units_grad_0, x_grad_0, last_units_1, gate_0))
    half_units_0 = scatter_halve(blocks_units_0)
    last_attn_1 = scatter_last(after(half_attn_1, x_grad_0, last_units_1))
    second_units = scatter_join(last_units_1, True)

    held = after((keep_1, send_1), attn_grad_1, sent_back)
    branch_1 = pair_sum(chip_sum(*held))
    output = own_places(block_result(middle_1, branch_1, biases_1, mods_1), all_frames)
    gate_1 = gate_sums(after(upstream_1, parts[0]), branch_1, biases_1, mods_1)

    input_sums_0 = after(input_sums_0, blocks_units_0, half_attn_1)
    packed_sums = pack_sums(
        clip_count,
        lax.axis_index("dp") * frames_dev,
        (
            (input_sums_0, middle_sums_0, gate_0, turn_sums_0, joined_bias_0, fc1_bias_0),
            (input_sums_1, middle_sums_1, gate_1, turn_sums_1, joined_bias_1, fc1_bias_1),
        ),
    )
    owned = jnp.sum(deal(packed_sums.reshape(all_devices, -1)), axis=0)
    near_sums = scatter_near_sums(after(start_attn_0, blocks_units_0, owned))
    near_attn_grad_0 = scatter_near(near_sums)
    held = after(owned, near_sums)
    everything = deal(jnp.broadcast_to(held[None], (all_devices, owned.shape[0])))
    held = after(near_attn_grad_0, everything, last_attn_1, half_units_0)
    sums_attn_0 = scatter_planes(scatter_plane_blocks(held))
    held = after(half_units_0, near_attn_grad_0, everything)
    first_units = scatter_join(scatter_last(held), True)
    second_attn = scatter_join(after(last_attn_1, near_attn_grad_0, everything))[0]
    first_attn = scatter_finish(sums_attn_0)
    everything = after(everything, sums_attn_0[0]).reshape(2, -1, width)
    mod_rows = 6 * clip_count
    summed_mod = everything[:, :mod_rows].reshape(2, clip_count, 6, width)
    b_ada_grad = lax.dynamic_slice_in_dim(jnp.sum(summed_mod, axis=1), own_start, own_width, 2)
    columns = everything[:, mod_rows + 2 : mod_rows + 6].reshape(2, 2, 2, width)[..., :head_width]
    proj_rows = jnp.concatenate(
        [
            jnp.concatenate([columns[:, 0], columns[:, 1]], axis=-1),
            everything[:, mod_rows : mod_rows + 2],
        ],
        axis=1,
    )
    b_proj_grad = lax.dynamic_slice_in_dim(proj_rows, own_start, own_width, 2)
    fc1_rows = everything[:, mod_rows + 6 :].reshape(2, -1)
    own_units = fc1_rows.shape[1] // all_devices
    b_fc1_grad = lax.dynamic_slice_in_dim(fc1_rows, flat_index * own_units, own_units, 1)
    w_ada_grad = sum(
        gated_own[clip][None, :, None, None] * summed_mod[:, clip][:, None]
        for clip in range(clip_count)
    )
    silu_grad = jnp.stack(
        [
            jnp.sum(summed_mod[:, clip][:, None] * w_ada_wide, axis=(0, 2, 3))
            for clip in range(clip_count)
        ]
    )
    cond_own = lax.dynamic_slice_in_dim(cond_float, own_start, own_width, 1)
    cond_grad = jax.vjp(jax.nn.silu, cond_own)[1](silu_grad)[0]

    reduced = ((first_attn, first_units), (second_attn, second_units))
    out_start = padded(joined_width)
    w_qkv_grad = jnp.stack(
        [part[0][:, :joined_width].reshape(own_rows, 3, head_width) for part in reduced]
    )
    w_out_grad = jnp.stack(
        [part[0][:, out_start : out_start + head_width].T for part in reduced]
    )
    w_fc1_grad = jnp.stack(
        [jnp.concatenate([part[1][0, :, :units], part[1][1, :, :units]], axis=1) for part in reduced]
    )
    w_fc2_grad = jnp.stack(
        [part[1][:, :, units:].transpose(0, 2, 1).reshape(2 * units, own_rows) for part in reduced]
    )
    return (
        output,
        tokens_grad,
        cond_grad,
        w_qkv_grad,
        w_out_grad,
        w_fc1_grad,
        w_fc2_grad,
        w_ada_grad,
        b_ada_grad,
        b_proj_grad,
        b_fc1_grad,
    )


def solution(mesh):
    return jax.shard_map(
        per_device,
        mesh=mesh,
        in_specs=(
            P("dp", "tensor", None, None),
            P(),
            P(None, "tensor", "dp", None),
            P(None, "dp", None, "tensor"),
            P(None, "tensor", "dp"),
            P(None, "dp", "tensor"),
            P(None, "tensor", "dp"),
            P(None, ("dp", "tensor"), None, None),
            P(None, None, ("dp", "tensor")),
            P(None, None, ("dp", "tensor")),
            P(None, ("dp", "tensor")),
        ),
        out_specs=(
            P(None, "tensor", "dp", None),
            P("dp", "tensor", None, None),
            P(None, ("dp", "tensor")),
            P(None, "dp", None, "tensor"),
            P(None, "tensor", "dp"),
            P(None, "dp", "tensor"),
            P(None, "tensor", "dp"),
            P(None, ("dp", "tensor"), None, None),
            P(None, None, ("dp", "tensor")),
            P(None, None, ("dp", "tensor")),
            P(None, ("dp", "tensor")),
        ),
        check_vma=False,
    )
```
